256 devices in a mesh: seq: 64 (over z, x, core), vol: 4 (over y).
Axes of the slice: x: 4, y: 4, z: 8, core: 2. Of those that a mesh axis runs over, the one named last changes fastest.
Arguments:
- x_raw: bfloat16 [65536, 4096], P(('vol', 'seq')), parts along dimension 0, may hold values from -6 to 6
- z_gate: bfloat16 [65536, 4096], P(('vol', 'seq')), parts along dimension 0, may hold values from -6 to 6
- bc_raw: bfloat16 [65536, 256], P(('vol', 'seq')), parts along dimension 0, may hold values from -6 to 6
- dt_raw: bfloat16 [65536, 64], P(('vol', 'seq')), parts along dimension 0, may hold values from -5 to 5
- conv_x: float32 [4, 4096], replicated, may hold values from -3 to 3
- conv_x_bias: float32 [4096], replicated, may hold values from -0.5 to 0.5
- conv_bc: float32 [4, 256], replicated, may hold values from -3 to 3
- conv_bc_bias: float32 [256], replicated, may hold values from -0.5 to 0.5
- dt_bias: float32 [64], replicated, may hold values from -3 to 0
- a_log: float32 [64], replicated, may hold values from -11 to -2
- skip_gain: float32 [64], replicated, may hold values from 0.5 to 1.5
- norm_gain: float32 [4096], replicated, may hold values from 0.5 to 1.5
Outputs:
- mixed: bfloat16 [65536, 4096], P(('vol', 'seq')), parts along dimension 0
The draws below stay inside these ranges and needn't reach their ends.
There are 4 independent parts, one for each index of `vol`. The reference program is written for one: setup_inputs(seed, part) draws one part's arguments, and reference() takes and returns one part's arrays. A program takes and returns all parts, laid end to end along the dimension named above; an argument that names none is the same for every part. Nothing has to cross between parts.
All inputs are finite; a program needn't handle non-finite values.
Results may differ from the reference program's by a relative error of at most 0.0055.
Values may be sent and summed in bfloat16 or wider, within the bound.
A program may use at most 192 MiB of HBM per device.

```python
import jax
import jax.numpy as jnp
from jax import lax

P_SIZE = 64
N = 128
H = 64
DI = 4096
KCONV = 4
Q = 256
TOKENS = 16384


def block_scale(rng, extent, shards, smallest, largest):
    factor_of = 1.0
    for axis_at, shards_of in shards:
        steps = jax.random.uniform(jax.random.fold_in(jax.random.fold_in(rng, 6), axis_at), (shards_of,), jnp.float32, smallest / len(shards), largest / len(shards))
        factor_of = factor_of * jnp.repeat(jnp.exp(steps), extent[axis_at] // shards_of).reshape((-1,) + (1,) * (len(extent) - 1 - axis_at))
    return factor_of


def centred(own_key, extent, scale, most, shards=(), dtype=jnp.bfloat16):
    array = scale * jax.random.normal(own_key, extent, jnp.float32)
    if shards:
        array = array * block_scale(own_key, extent, shards, -0.22, 0.18)
    return jnp.clip(array, -most, most).astype(dtype)


def setup_inputs(seed: int = 0, part: int = 0) -> dict:
    key_list = jax.random.split(jax.random.key(seed), 13)
    part_keys = jax.random.split(jax.random.fold_in(key_list[12], part), 13)
    x_raw = centred(part_keys[0], (TOKENS, DI), 1.0, 6.0, ((0, 64),))
    z_gate = centred(part_keys[1], (TOKENS, DI), 1.0, 6.0, ((0, 64),))
    bc_raw = centred(part_keys[2], (TOKENS, 2 * N), 1.0, 6.0, ((0, 64),))
    dt_raw = centred(part_keys[3], (TOKENS, H), 1.0, 5.0, ((0, 64),))
    conv_x = centred(key_list[4], (KCONV, DI), KCONV ** -0.5, 3.0, (), jnp.float32)
    conv_x_bias = jnp.clip(jax.random.uniform(key_list[5], (DI,), jnp.float32, -0.5, 0.5), -0.5, 0.5)
    conv_bc = centred(key_list[6], (KCONV, 2 * N), KCONV ** -0.5, 3.0, (), jnp.float32)
    conv_bc_bias = jnp.clip(jax.random.uniform(key_list[7], (2 * N,), jnp.float32, -0.5, 0.5), -0.5, 0.5)
    dt_bias = jnp.clip(jax.random.uniform(key_list[8], (H,), jnp.float32, -3.0, 0.0), -3.0, 0.0)
    a_log = jnp.clip(jax.random.uniform(key_list[9], (H,), jnp.float32, -11.0, -2.0), -11.0, -2.0)
    skip_gain = jnp.clip(jax.random.uniform(key_list[10], (H,), jnp.float32, 0.5, 1.5), 0.5, 1.5)
    norm_gain = jnp.clip(1.0 + 0.1 * jax.random.normal(key_list[11], (DI,), jnp.float32), 0.5, 1.5)
    return {"x_raw": x_raw, "z_gate": z_gate, "bc_raw": bc_raw, "dt_raw": dt_raw, "conv_x": conv_x, "conv_x_bias": conv_x_bias, "conv_bc": conv_bc, "conv_bc_bias": conv_bc_bias, "dt_bias": dt_bias, "a_log": a_log, "skip_gain": skip_gain, "norm_gain": norm_gain}


def round_bf(value):
    return lax.optimization_barrier(value.astype(jnp.bfloat16))

def conv_silu(source, weight, offset):
    tok_rows = source.shape[0]
    padded = jnp.pad(source.astype(jnp.float32), ((KCONV - 1, 0), (0, 0)))
    acc = offset[None, :] + jnp.zeros((tok_rows, source.shape[1]), jnp.float32)
    for tap in range(KCONV):
        acc = acc + weight[tap][None, :] * padded[tap:tap + tok_rows]
    return jax.nn.silu(acc).astype(jnp.bfloat16)

def reference(x_raw, z_gate, bc_raw, dt_raw, conv_x, conv_x_bias, conv_bc, conv_bc_bias, dt_bias, a_log, skip_gain, norm_gain):
    blocks = TOKENS // Q
    x_conv = conv_silu(x_raw, conv_x, conv_x_bias).reshape(blocks, Q, H, P_SIZE)
    bc_conv = conv_silu(bc_raw, conv_bc, conv_bc_bias)
    b_mat = bc_conv[:, :N].reshape(blocks, Q, N)
    c_mat = bc_conv[:, N:].reshape(blocks, Q, N)
    step_size = jax.nn.softplus(dt_raw.astype(jnp.float32) + dt_bias[None, :])
    rate = -jnp.exp(a_log)[None, :] * step_size
    log_decay = jnp.cumsum(rate.reshape(blocks, Q, H), axis=1)
    step_size = step_size.reshape(blocks, Q, H)
    later_mask = (lax.broadcasted_iota(jnp.int32, (Q, Q), 0) >= lax.broadcasted_iota(jnp.int32, (Q, Q), 1))[:, :, None]

    def advance(state, inputs):
        x_block, step_block, decay_block, b_block, c_block = inputs
        x_wide = x_block.astype(jnp.float32)
        last_log = decay_block[-1]
        scores = jnp.dot(c_block, b_block.T, preferred_element_type=jnp.float32)
        gap_log = decay_block[:, None, :] - decay_block[None, :, :]
        mixing = round_bf(scores[:, :, None] * jnp.exp(jnp.where(later_mask, gap_log, -jnp.inf)) * step_block[None, :, :])
        inside = jnp.einsum('tsh,shp->thp', mixing.astype(jnp.float32), x_wide)
        carried = jnp.einsum('tn,hpn->thp', c_block.astype(jnp.float32), round_bf(state).astype(jnp.float32))
        y_block = inside + jnp.exp(decay_block)[:, :, None] * carried + skip_gain[None, :, None] * x_wide
        weighted = round_bf(x_wide * (step_block * jnp.exp(last_log[None, :] - decay_block))[:, :, None])
        block_state = jnp.einsum('shp,sn->hpn', weighted.astype(jnp.float32), b_block.astype(jnp.float32))
        new_state = jnp.exp(last_log)[:, None, None] * state + block_state
        return (new_state, y_block.astype(jnp.bfloat16))
    start_state = jnp.zeros((H, P_SIZE, N), jnp.float32)
    _, y_all = lax.scan(advance, start_state, (x_conv, step_size, log_decay, b_mat, c_mat))
    y_all = y_all.reshape(TOKENS, DI).astype(jnp.float32)
    gated = y_all * jax.nn.silu(z_gate.astype(jnp.float32))
    mean_sq = lax.optimization_barrier(jnp.mean(gated * gated, axis=1, keepdims=True))
    return (gated * lax.rsqrt(mean_sq + 1e-05) * norm_gain[None, :]).astype(jnp.bfloat16)
```

```python
import functools

import jax
import jax.numpy as jnp
from jax import lax
from jax.experimental import pallas as pl
from jax.experimental.pallas import tpu as pltpu
from jax.sharding import PartitionSpec as P

T = 256
N = 128
HL = 64
LOG2E = 1.4426950408889634
F32 = jnp.float32
BF16 = jnp.bfloat16


def dot(a, b):
    return jnp.dot(a, b, preferred_element_type=F32)


def silu(v):
    return v / (1.0 + jnp.exp(-v))


def kernel(
    nz,
    nx,
    di,
    nk,
    x_hbm,
    z_hbm,
    bc_ref,
    dt_ref,
    wx_ref,
    bx_ref,
    wbc_ref,
    bbc_ref,
    dtb_ref,
    alog_ref,
    skip_ref,
    gain_ref,
    out_hbm,
    xv,
    zv,
    xc,
    halo_x,
    halo_bc,
    dtw,
    ex,
    ldg,
    rt,
    f1s,
    f2s,
    bt,
    cm,
    sc,
    skw,
    inside,
    ssq,
    ov,
    lo_b,
    lp_b,
    cl_b,
    xd_b,
    pl_b,
    zd_b,
    dx,
    dl,
    dz,
    sbf,
    srecv,
    csb,
    xrecv,
    ptb,
    zrecv,
    pesend,
    perecv,
    esend,
    erecv,
    entsend,
    ent,
    sem_in,
    sem_out,
    sem_halo,
    sem_l,
    sx_s,
    sx_r,
    sz_s,
    sz_r,
    d_s,
    d_r,
    x_s,
    x_r,
    z_s,
    z_r,
    zb_s,
    zb_r,
    xb_s,
    xb_r,
    db_s,
    db_r,
):
    ch = di // nk
    zw = ch // nz
    hr = N // 2
    xr = hr // nx
    ngroup = di // 512

    me = lax.axis_index("seq")
    c = lax.rem(me, 2)
    x = lax.rem(me // 2, nx)
    z = me // (2 * nx)
    nseq = 2 * nx * nz

    def at(zz, xx, cc):
        return (zz * nx + xx) * 2 + cc

    partner = at(z, x, 1 - c)
    nxt = lax.rem(me + 1, nseq)
    prv = lax.rem(me + nseq - 1, nseq)
    xpeer = [lax.rem(x + d, nx) for d in range(1, nx)]
    zpeer = [lax.rem(z + d, nz) for d in range(1, nz)]

    barrier = pltpu.get_barrier_semaphore()
    peers = [partner, nxt, prv]
    peers += [at(z, xp, c) for xp in xpeer]
    peers += [at(zp, x, c) for zp in zpeer]
    for p in peers:
        pl.semaphore_signal(barrier, inc=1, device_id={"seq": p})

    def rcopy(src, dst, ss, rs, dev):
        return pltpu.make_async_remote_copy(
            src_ref=src, dst_ref=dst, send_sem=ss, recv_sem=rs, device_id={"seq": dev}
        )

    half = di // 2
    cols = [pl.ds(0, half), pl.ds(half, half)]
    xin = [pltpu.make_async_copy(x_hbm.at[:, q], xv.at[:, q], sem_in.at[i]) for i, q in enumerate(cols)]
    zin = pltpu.make_async_copy(z_hbm, zv, sem_in.at[2])
    for cp in xin:
        cp.start()
    zin.start()

    dtw[:, 0:HL] = dt_ref[...].astype(F32) + dtb_ref[...]
    dtw[:, HL : 2 * HL] = dt_ref[...].astype(F32) + dtb_ref[...]
    lo_b[:, 0:HL] = jnp.broadcast_to(jnp.exp(alog_ref[...]), (8, HL))
    lo_b[:, HL : 2 * HL] = jnp.broadcast_to(jnp.exp(alog_ref[...]), (8, HL))
    arate = lo_b[0:1, :]
    lo_b[:, 0:HL] = jnp.broadcast_to(skip_ref[...], (8, HL))
    lo_b[:, HL : 2 * HL] = jnp.broadcast_to(skip_ref[...], (8, HL))
    skipd = lo_b[...]
    raw = dtw[...]
    step = jnp.maximum(raw, 0.0) + jnp.log1p(jnp.exp(-jnp.abs(raw)))
    rate = -arate * step
    low = lax.broadcasted_iota(jnp.int32, (T, T), 0) >= lax.broadcasted_iota(jnp.int32, (T, T), 1)
    ld2 = jnp.dot(
        jnp.where(low, 1.0, 0.0),
        rate,
        precision=lax.Precision.HIGHEST,
        preferred_element_type=F32,
    ) * LOG2E
    r2 = ld2 - jnp.log(step) * LOG2E
    last2 = ld2[T - 1 : T, :]

    def pair(v):
        hi = v.astype(BF16).astype(F32)
        lane = lax.broadcasted_iota(jnp.int32, v.shape, 1)
        return jnp.where(lane < HL, hi, v - hi).astype(BF16)

    f1s[...] = pair(jnp.exp2(last2 - r2))
    f2s[...] = pair(jnp.exp2(ld2))
    rt[...] = jnp.transpose(r2)
    for g in range(ngroup):
        ldg[g] = ld2 if g == 0 else pltpu.roll(ld2, 128 - 8 * g, axis=1)
    lo_b[...] = jnp.broadcast_to(last2, (8, 2 * HL))

    @pl.loop(0, ngroup)
    def _(g):
        row = lax.broadcasted_iota(jnp.int32, (128, 512), 0) & 63
        head = (lax.broadcasted_iota(jnp.int32, (128, 512), 1) >> 6) + g * 8
        lanes = pl.ds(pl.multiple_of(g * 512, 512), 512)
        ex[:, lanes] = jnp.where(row == head, 1.0, 0.0).astype(BF16)
        skw[:, lanes] = dot(pair(jnp.concatenate([skipd, skipd], 0)), ex[:, lanes])[0:8]

    pl.semaphore_wait(barrier, len(peers))
    hal = [
        rcopy(x_hbm.at[pl.ds(T - 8, 8), :], halo_x, sem_halo.at[0], sem_halo.at[1], nxt),
        rcopy(bc_ref.at[pl.ds(T - 8, 8), :], halo_bc, sem_halo.at[2], sem_halo.at[3], nxt),
    ]
    for cp in hal:
        cp.start()
    lcopy = rcopy(lo_b, lp_b, sem_l.at[0], sem_l.at[1], partner)
    lcopy.start()

    def conv_main(src, dst, w_ref, b_ref, lanes):
        v = src[:, lanes].astype(F32)
        acc = b_ref[:, lanes] + w_ref[3:4, lanes] * v
        for k in range(1, 4):
            acc = acc + w_ref[3 - k : 4 - k, lanes] * pltpu.roll(v, k, axis=0)
        dst[:, lanes] = silu(acc).astype(BF16)

    def conv_head(src, halo, w_ref, b_ref, lanes):
        top = jnp.where(me > 0, halo[:, lanes].astype(F32), 0.0)
        v = jnp.concatenate([top, src[0:16, lanes].astype(F32)], axis=0)
        acc = b_ref[:, lanes] + w_ref[3:4, lanes] * v
        for k in range(1, 4):
            acc = acc + w_ref[3 - k : 4 - k, lanes] * pltpu.roll(v, k, axis=0)
        return silu(acc[8:24]).astype(BF16)

    for i in range(2):
        xin[i].wait()

        @pl.loop(0, half // 256)
        def _(j):
            conv_main(xv, xc, wx_ref, bx_ref, pl.ds(pl.multiple_of(i * half + j * 256, 256), 256))

    for cp in hal:
        cp.wait_recv()

    @pl.loop(0, di // 512)
    def _(j):
        lanes = pl.ds(pl.multiple_of(j * 512, 512), 512)
        xc[0:16, lanes] = conv_head(xv, halo_x, wx_ref, bx_ref, lanes)

    whole = pl.ds(0, 2 * N)
    bcs = ov.at[:, pl.ds(0, 2 * N)]
    conv_main(bc_ref, bcs, wbc_ref, bbc_ref, whole)
    bcs[0:16, :] = conv_head(bc_ref, halo_bc, wbc_ref, bbc_ref, whole)
    bm = bcs[:, 0:N]
    cm[...] = bcs[:, N : 2 * N]
    bt[...] = jnp.transpose(bm.astype(F32)).astype(BF16)

    lcopy.wait_recv()
    own = lo_b[...]
    other = lp_b[...]
    first = c == 0
    l0 = jnp.where(first, own, other)
    l1 = jnp.where(first, other, own)
    cl = l0 + l1
    cl_b[...] = cl
    xd_b[x] = cl
    dxs = [rcopy(cl_b, xd_b.at[x], sx_s.at[d], sx_r.at[x], at(z, xp, c)) for d, xp in enumerate(xpeer)]
    for cp in dxs:
        cp.start()
    dl[...] = dot(
        pair(jnp.concatenate([jnp.exp2(l0), jnp.exp2(l1)], axis=0)), ex[...]
    )

    def lanes_of(k):
        return pl.ds(k * ch, ch)

    oh = pl.multiple_of(c * hr, hr)
    ph = pl.multiple_of((1 - c) * hr, hr)

    def d_copy(k):
        return rcopy(
            sbf.at[pl.ds(ph, hr), lanes_of(k)], srecv.at[:, lanes_of(k)], d_s.at[k], d_r.at[k], partner
        )

    def stage_a(k):
        for j in range(ch // 256):
            lanes = pl.ds(k * ch + j * 256, 256)
            f1e = dot(f1s[...], ex[:, lanes])
            weighted = (xc[:, lanes].astype(F32) * f1e).astype(BF16)
            sbf[:, lanes] = dot(bt[...], weighted).astype(BF16)
        d_copy(k).start()

    def x_copy(k, d):
        xp = xpeer[d]
        rows = pl.ds(pl.multiple_of(xp * xr, xr), xr)
        return rcopy(
            csb.at[rows, lanes_of(k)],
            xrecv.at[x, :, lanes_of(k)],
            x_s.at[k, d],
            x_r.at[k, x],
            at(z, xp, c),
        )

    def x_wait(k, d):
        xp = xpeer[d]
        rcopy(
            csb.at[pl.ds(0, xr), lanes_of(k)],
            xrecv.at[xp, :, lanes_of(k)],
            x_s.at[k, d],
            x_r.at[k, xp],
            at(z, xp, c),
        ).wait_recv()

    def stage_b(k):
        d_copy(k).wait_recv()
        lanes = lanes_of(k)
        mine = sbf[pl.ds(oh, hr), lanes].astype(F32)
        got = srecv[:, lanes].astype(F32)
        e1 = dl[8:9, lanes]
        wm = jnp.where(first, e1, 1.0)
        wg = jnp.where(first, 1.0, e1)
        csb[:, lanes] = (wm * mine + wg * got).astype(BF16)
        for d in range(nx - 1):
            x_copy(k, d).start()
        xrecv[x, :, lanes] = csb[pl.ds(pl.multiple_of(x * xr, xr), xr), lanes]

    def stage_decay_x():
        for d, xp in enumerate(xpeer):
            rcopy(cl_b, xd_b.at[xp], sx_s.at[d], sx_r.at[xp], at(z, xp, c)).wait_recv()
        rows = [xd_b[i][0:1] for i in range(nx)]
        total = rows[0]
        for i in range(1, nx):
            total = total + rows[i]
        after = []
        run = jnp.zeros_like(rows[0])
        for i in reversed(range(nx)):
            after.insert(0, run)
            run = run + rows[i]
        full = jnp.concatenate(
            after + rows + [jnp.zeros_like(rows[0])] * (16 - 2 * nx), axis=0
        )
        dx[...] = dot(pair(jnp.exp2(full)), ex[...])
        pl_b[...] = jnp.broadcast_to(total, (8, 2 * HL))
        zd_b[z] = jnp.broadcast_to(total, (8, 2 * HL))
        for d, zp in enumerate(zpeer):
            rcopy(pl_b, zd_b.at[z], sz_s.at[d], sz_r.at[z], at(zp, x, c)).start()

    def stage_decay_z():
        for d, zp in enumerate(zpeer):
            rcopy(pl_b, zd_b.at[zp], sz_s.at[d], sz_r.at[zp], at(zp, x, c)).wait_recv()
        full = jnp.concatenate(
            [zd_b[i][0:1] for i in range(nz)] + [jnp.zeros((16 - nz, 2 * HL), F32)], axis=0
        )
        full = pair(jnp.exp2(full))
        for k in range(nk):
            lanes = pl.ds(pl.multiple_of(k * ch + z * zw, zw), zw)
            dz[:, k * zw : (k + 1) * zw] = dot(full, ex[:, lanes])

    def z_copy(k, d):
        zp = zpeer[d]
        src = ptb.at[:, pl.ds(pl.multiple_of(k * ch + zp * zw, zw), zw)]
        return rcopy(
            src, zrecv.at[z, :, pl.ds(k * zw, zw)], z_s.at[k, d], z_r.at[k, z], at(zp, x, c)
        )

    def stage_c(k):
        for d in range(nx - 1):
            x_wait(k, d)
        lanes = lanes_of(k)
        tot = dx[0:1, lanes] * xrecv[0, :, lanes].astype(F32)
        for i in range(1, nx):
            tot = tot + dx[i : i + 1, lanes] * xrecv[i, :, lanes].astype(F32)
        ptb[:, lanes] = tot.astype(BF16)
        for d in range(nz - 1):
            z_copy(k, d).start()
        zrecv[z, :, pl.ds(k * zw, zw)] = ptb[:, pl.ds(pl.multiple_of(k * ch + z * zw, zw), zw)]

    def zb_copy(k, d):
        zp = zpeer[d]
        lanes = pl.ds(pl.multiple_of(k * ch + z * zw, zw), zw)
        return rcopy(
            pesend.at[zp, :, pl.ds(k * zw, zw)],
            perecv.at[:, lanes],
            zb_s.at[k, d],
            zb_r.at[k, z],
            at(zp, x, c),
        )

    def stage_d(k):
        own_lanes = pl.ds(k * zw, zw)
        for d, zp in enumerate(zpeer):
            rcopy(
                ptb.at[:, pl.ds(0, zw)],
                zrecv.at[zp, :, own_lanes],
                z_s.at[k, d],
                z_r.at[k, zp],
                at(zp, x, c),
            ).wait_recv()
        state = jnp.zeros((xr, zw), F32)
        for i in range(nz):
            pesend[i, :, own_lanes] = state.astype(BF16)
            state = dz[i : i + 1, own_lanes] * state + zrecv[i, :, own_lanes].astype(F32)
        for d in range(nz - 1):
            zb_copy(k, d).start()
        perecv[:, pl.ds(pl.multiple_of(k * ch + z * zw, zw), zw)] = pesend[z, :, own_lanes]

    def xb_copy(k, d):
        xp = xpeer[d]
        rows = pl.ds(pl.multiple_of(x * xr, xr), xr)
        return rcopy(
            esend.at[xp, :, lanes_of(k)],
            erecv.at[rows, lanes_of(k)],
            xb_s.at[k, d],
            xb_r.at[k, x],
            at(z, xp, c),
        )

    def stage_e(k):
        for d, zp in enumerate(zpeer):
            lanes = pl.ds(pl.multiple_of(k * ch + zp * zw, zw), zw)
            rcopy(
                pesend.at[zp, :, pl.ds(k * zw, zw)],
                perecv.at[:, lanes],
                zb_s.at[k, d],
                zb_r.at[k, zp],
                at(zp, x, c),
            ).wait_recv()
        lanes = lanes_of(k)
        state = perecv[:, lanes].astype(F32)
        for i in range(nx):
            esend[i, :, lanes] = state.astype(BF16)
            if i < nx - 1:
                state = dx[nx + i : nx + i + 1, lanes] * state + xrecv[i, :, lanes].astype(F32)
        for d in range(nx - 1):
            xb_copy(k, d).start()
        erecv[pl.ds(pl.multiple_of(x * xr, xr), xr), lanes] = esend[x, :, lanes]

    def db_copy(k):
        return rcopy(
            entsend.at[:, lanes_of(k)],
            ent.at[pl.ds(oh, hr), lanes_of(k)],
            db_s.at[k],
            db_r.at[k],
            partner,
        )

    def stage_f(k):
        lanes = lanes_of(k)
        for d, xp in enumerate(xpeer):
            rows = pl.ds(pl.multiple_of(xp * xr, xr), xr)
            rcopy(
                esend.at[xp, :, lanes],
                erecv.at[rows, lanes],
                xb_s.at[k, d],
                xb_r.at[k, xp],
                at(z, xp, c),
            ).wait_recv()
        e0 = erecv[:, lanes]
        mine = sbf[pl.ds(oh, hr), lanes]
        got = srecv[:, lanes]
        s0 = jnp.where(first, mine, got).astype(F32)
        e1 = (dl[0:1, lanes] * e0.astype(F32) + s0).astype(BF16)
        entsend[:, lanes] = jnp.where(first, e1, e0)
        db_copy(k).start()
        ent[pl.ds(oh, hr), lanes] = jnp.where(first, e0, e1)

    def scores():
        s = lax.dot_general(
            cm[...], bcs[:, 0:N], (((1,), (1,)), ((), ())), preferred_element_type=F32
        )
        low_mask = lax.broadcasted_iota(jnp.int32, (T, T), 0) >= lax.broadcasted_iota(
            jnp.int32, (T, T), 1
        )
        sc[...] = jnp.where(low_mask, s, 0.0)

    hb = T // 2

    def mix_group(g):
        ldt = ldg[g]
        rtile = rt[pl.ds(pl.multiple_of(g * 8, 8), 8), :]
        for j in range(4):
            lanes = pl.ds(pl.multiple_of(g * 512 + j * 128, 128), 128)
            xp = xc[:, lanes]
            lane = lax.broadcasted_iota(jnp.int32, (T, 128), 1)
            xa = jnp.where(lane < 64, xp.astype(F32), 0.0).astype(BF16)
            xb = jnp.where(lane >= 64, xp.astype(F32), 0.0).astype(BF16)
            tops = []
            bots = []
            for a in range(2):
                i = 2 * j + a
                col = ldt[:, i : i + 1]
                row = rtile[i : i + 1, :]
                tl = jnp.exp2(jnp.minimum(col[0:hb] - row[:, 0:hb], 126.0)) * sc[0:hb, 0:hb]
                bl = jnp.exp2(col[hb:T] - row[:, 0:hb]) * sc[hb:T, 0:hb]
                br = jnp.exp2(jnp.minimum(col[hb:T] - row[:, hb:T], 126.0)) * sc[hb:T, hb:T]
                tops.append(tl.astype(BF16))
                bots += [bl.astype(BF16), br.astype(BF16)]
            yt = dot(jnp.concatenate(tops, 1), jnp.concatenate([xa[0:hb], xb[0:hb]], 0))
            yb = dot(jnp.concatenate(bots, 1), jnp.concatenate([xa, xb], 0))
            sk = skw[0:1, lanes] * xp.astype(F32)
            inside[0:hb, lanes] = yt + sk[0:hb]
            inside[hb:T, lanes] = yb + sk[hb:T]

    def stage_g(k):
        db_copy(k).wait_recv()

        @pl.loop(0, ch // 256)
        def _(j):
            lanes = pl.ds(pl.multiple_of(k * ch + j * 256, 256), 256)
            f2e = dot(f2s[...], ex[:, lanes])
            y = (inside[:, lanes] + f2e * dot(cm[...], ent[:, lanes])).astype(BF16)
            gated = y.astype(F32) * silu(zv[:, lanes].astype(F32))
            inside[:, lanes] = gated
            sq = gated * gated
            ssq[...] += sq[:, 0:128] + sq[:, 128:256]

    stage_a(0)
    stage_a(1)
    stage_b(0)
    for k in range(2, nk):
        stage_a(k)
        stage_b(k - 1)
    stage_decay_x()
    stage_b(nk - 1)
    scores()
    ssq[...] = jnp.zeros_like(ssq)
    zin.wait()

    fill = list(range(ngroup))

    def filler():
        if fill:
            g = fill.pop(0)
            mix_group(g)

    for s in range(nk):
        filler()
        stage_c(s)
    stage_decay_z()
    for s in range(nk):
        filler()
        stage_d(s)
    while fill:
        filler()
    for s in range(nk):
        stage_e(s)
    for s in range(nk):
        stage_f(s)
    for s in range(nk):
        stage_g(s)

    ms = jnp.sum(ssq[...], axis=1, keepdims=True) * (1.0 / di)
    rs = lax.rsqrt(ms + 1e-05)
    outs = []
    for i in range(nk):

        @pl.loop(0, ch // 256)
        def _(j):
            lanes = pl.ds(pl.multiple_of(i * ch + j * 256, 256), 256)
            ov[:, lanes] = (inside[:, lanes] * rs * gain_ref[:, lanes]).astype(BF16)

        cp = pltpu.make_async_copy(ov.at[:, lanes_of(i)], out_hbm.at[:, lanes_of(i)], sem_out.at[i])
        cp.start()
        outs.append(cp)

    for cp in hal:
        cp.wait_send()
    lcopy.wait_send()
    for d in range(nx - 1):
        dxs[d].wait_send()
    for d, zp in enumerate(zpeer):
        rcopy(pl_b, zd_b.at[z], sz_s.at[d], sz_r.at[z], at(zp, x, c)).wait_send()
    for k in range(nk):
        d_copy(k).wait_send()
        db_copy(k).wait_send()
        for d in range(nx - 1):
            x_copy(k, d).wait_send()
            xb_copy(k, d).wait_send()
        for d in range(nz - 1):
            z_copy(k, d).wait_send()
            zb_copy(k, d).wait_send()
    for cp in outs:
        cp.wait()


def make_body(nz, nx, nk):
    def body(x_raw, z_gate, bc_raw, dt_raw, wx, bx, wbc, bbc, dtb, alog, skip, gain):
        di = x_raw.shape[1]
        ch = di // nk
        zw = ch // nz
        hr = N // 2
        xr = hr // nx
        ng = di // 512
        vm = lambda *s: pltpu.VMEM(s, F32)
        vb = lambda *s: pltpu.VMEM(s, BF16)
        dma = lambda *s: pltpu.SemaphoreType.DMA(s)
        anyspec = pl.BlockSpec(memory_space=pl.ANY)
        vspec = pl.BlockSpec(memory_space=pltpu.VMEM)
        scratch = [
            vb(T, di),
            vb(T, di),
            vb(T, di),
            vb(8, di),
            vb(8, 2 * N),
            vm(T, 128),
            vb(128, di),
            vm(ng, T, 128),
            vm(128, T),
            vb(T, 128),
            vb(T, 128),
            vb(N, T),
            vb(T, N),
            vm(T, T),
            vm(8, di),
            vm(T, di),
            vm(T, 128),
            vb(T, di),
            vm(8, 128),
            vm(8, 128),
            vm(8, 128),
            vm(nx, 8, 128),
            vm(8, 128),
            vm(nz, 8, 128),
            vm(16, di),
            vm(16, di),
            vm(16, nk * zw),
            vb(N, di),
            vb(hr, di),
            vb(hr, di),
            vb(nx, xr, di),
            vb(xr, di),
            vb(nz, xr, nk * zw),
            vb(nz, xr, nk * zw),
            vb(xr, di),
            vb(nx, xr, di),
            vb(hr, di),
            vb(hr, di),
            vb(N, di),
            dma(3),
            dma(nk),
            dma(4),
            dma(2),
            dma(nx),
            dma(nx),
            dma(nz),
            dma(nz),
            dma(nk),
            dma(nk),
            dma(nk, nx),
            dma(nk, nx),
            dma(nk, nz),
            dma(nk, nz),
            dma(nk, nz),
            dma(nk, nz),
            dma(nk, nx),
            dma(nk, nx),
            dma(nk),
            dma(nk),
        ]
        return pl.pallas_call(
            functools.partial(kernel, nz, nx, di, nk),
            out_shape=jax.ShapeDtypeStruct((T, di), BF16),
            in_specs=[anyspec, anyspec] + [vspec] * 10,
            out_specs=anyspec,
            scratch_shapes=scratch,
            compiler_params=pltpu.CompilerParams(
                collective_id=0, has_side_effects=True, vmem_limit_bytes=60 * 1024 * 1024
            ),
        )(
            x_raw,
            z_gate,
            bc_raw,
            dt_raw,
            wx,
            bx.reshape(1, -1),
            wbc,
            bbc.reshape(1, -1),
            dtb.reshape(1, -1),
            alog.reshape(1, -1),
            skip.reshape(1, -1),
            gain.reshape(1, -1),
        )

    return body


def solution(mesh):
    nx = 4
    nz = mesh.shape["seq"] // (2 * nx)
    tok = P(("vol", "seq"), None)
    return jax.shard_map(
        make_body(nz, nx, 4),
        mesh=mesh,
        in_specs=(tok, tok, tok, tok) + (P(),) * 8,
        out_specs=tok,
        check_vma=False,
    )
```

```python
import functools

import jax
import jax.numpy as jnp
from jax import lax
from jax.experimental import pallas as pl
from jax.experimental.pallas import tpu as pltpu
from jax.sharding import PartitionSpec as P

T = 256
N = 128
HL = 64
LOG2E = 1.4426950408889634
F32 = jnp.float32
BF16 = jnp.bfloat16


def dot(a, b):
    return jnp.dot(a, b, preferred_element_type=F32)


def silu(v):
    return v / (1.0 + jnp.exp(-v))


def kernel(
    nz,
    nx,
    di,
    nk,
    x_hbm,
    z_hbm,
    bc_hbm,
    dt_hbm,
    wx_hbm,
    bx_hbm,
    wbc_hbm,
    bbc_hbm,
    dtb_hbm,
    alog_hbm,
    skip_hbm,
    gain_hbm,
    out_hbm,
    bc_ref,
    dt_ref,
    wx_ref,
    bx_ref,
    wbc_ref,
    bbc_ref,
    dtb_ref,
    alog_ref,
    skip_ref,
    gain_ref,
    bcs,
    zs,
    xv,
    zv,
    xc,
    halo_x,
    halo_bc,
    r2s,
    ex,
    ldg,
    rt,
    f1s,
    f2s,
    bt,
    cm,
    sc,
    skw,
    inside,
    ssq,
    ov,
    lo_b,
    lp_b,
    cl_b,
    xd_b,
    pl_b,
    zd_b,
    dx,
    dl,
    dz,
    sbf,
    srecv,
    csb,
    xrecv,
    ptb,
    zrecv,
    pesend,
    perecv,
    esend,
    erecv,
    entsend,
    ent,
    sem_in,
    sem_small,
    sem_out,
    sem_halo,
    sem_l,
    sx_s,
    sx_r,
    sz_s,
    sz_r,
    d_s,
    d_r,
    x_s,
    x_r,
    z_s,
    z_r,
    zb_s,
    zb_r,
    xb_s,
    xb_r,
    db_s,
    db_r,
):
    ch = di // nk
    zw = ch // nz
    hr = N // 2
    xr = hr // nx
    ngroup = di // 512

    me = lax.axis_index("seq")
    c = lax.rem(me, 2)
    x = lax.rem(me // 2, nx)
    z = me // (2 * nx)
    nseq = 2 * nx * nz

    def at(zz, xx, cc):
        return (zz * nx + xx) * 2 + cc

    partner = at(z, x, 1 - c)
    nxt = lax.rem(me + 1, nseq)
    prv = lax.rem(me + nseq - 1, nseq)
    xpeer = [lax.rem(x + d, nx) for d in range(1, nx)]
    zpeer = [lax.rem(z + d, nz) for d in range(1, nz)]

    barrier = pltpu.get_barrier_semaphore()
    peers = [partner, nxt, prv]
    peers += [at(z, xp, c) for xp in xpeer]
    peers += [at(zp, x, c) for zp in zpeer]
    for p in peers:
        pl.semaphore_signal(barrier, inc=1, device_id={"seq": p})

    def rcopy(src, dst, ss, rs, dev):
        return pltpu.make_async_remote_copy(
            src_ref=src, dst_ref=dst, send_sem=ss, recv_sem=rs, device_id={"seq": dev}
        )

    def lanes_of(k):
        return pl.ds(k * ch, ch)

    smalls = [
        (dt_hbm, dt_ref),
        (dtb_hbm, dtb_ref),
        (alog_hbm, alog_ref),
        (bc_hbm, bc_ref),
        (wx_hbm, wx_ref),
        (bx_hbm, bx_ref),
        (wbc_hbm, wbc_ref),
        (bbc_hbm, bbc_ref),
        (skip_hbm, skip_ref),
        (gain_hbm, gain_ref),
    ]
    small_in = [pltpu.make_async_copy(p, q, sem_small.at[i]) for i, (p, q) in enumerate(smalls)]
    xin = [
        pltpu.make_async_copy(x_hbm.at[:, lanes_of(k)], xv.at[:, lanes_of(k)], sem_in.at[k])
        for k in range(nk)
    ]
    zin = pltpu.make_async_copy(z_hbm, zv, sem_in.at[nk])
    for cp in small_in[0:3]:
        cp.start()
    xin[0].start()
    for cp in small_in[3:]:
        cp.start()
    for cp in xin[1:]:
        cp.start()
    zin.start()

    def twice(ref):
        row = jnp.broadcast_to(ref[...], (8, HL))
        return jnp.concatenate([row, row], axis=1)

    for cp in small_in[0:3]:
        cp.wait()
    dtv = dt_ref[...].astype(F32)
    raw = jnp.transpose(jnp.concatenate([dtv, dtv], axis=0)) + twice(dtb_ref)[0:1]
    step = jnp.maximum(raw, 0.0) + jnp.log1p(jnp.exp(-jnp.abs(raw)))
    rate = -jnp.exp(twice(alog_ref)[0:1]) * step
    low = lax.broadcasted_iota(jnp.int32, (T, T), 0) >= lax.broadcasted_iota(jnp.int32, (T, T), 1)
    ld2 = jnp.dot(
        jnp.where(low, 1.0, 0.0),
        rate,
        precision=lax.Precision.HIGHEST,
        preferred_element_type=F32,
    ) * LOG2E
    r2 = ld2 - jnp.log(step) * LOG2E
    last2 = ld2[T - 1 : T, :]
    ldg[0] = ld2
    r2s[...] = r2

    def pair(v):
        hi = v.astype(BF16).astype(F32)
        lane = lax.broadcasted_iota(jnp.int32, v.shape, 1)
        return jnp.where(lane < HL, hi, v - hi).astype(BF16)

    f1s[...] = pair(jnp.exp2(last2 - r2))
    lo_b[...] = jnp.broadcast_to(last2, (8, 2 * HL))

    def make_ex(k):
        @pl.loop(0, ch // 256)
        def _(j):
            base = k * ch + j * 256
            row = lax.broadcasted_iota(jnp.int32, (128, 256), 0) & 63
            head = (lax.broadcasted_iota(jnp.int32, (128, 256), 1) + base) >> 6
            ex[:, pl.ds(pl.multiple_of(base, 256), 256)] = jnp.where(row == head, 1.0, 0.0).astype(BF16)

    pl.semaphore_wait(barrier, len(peers))
    hal = [
        rcopy(x_hbm.at[pl.ds(T - 8, 8), :], halo_x, sem_halo.at[0], sem_halo.at[1], nxt),
        rcopy(bc_hbm.at[pl.ds(T - 8, 8), :], halo_bc, sem_halo.at[2], sem_halo.at[3], nxt),
    ]
    for cp in hal:
        cp.start()
    lcopy = rcopy(lo_b, lp_b, sem_l.at[0], sem_l.at[1], partner)
    lcopy.start()

    def conv_main(src, dst, w_ref, b_ref, lanes):
        v = src[:, lanes].astype(F32)
        acc = b_ref[:, lanes] + w_ref[3:4, lanes] * v
        for k in range(1, 4):
            acc = acc + w_ref[3 - k : 4 - k, lanes] * pltpu.roll(v, k, axis=0)
        dst[:, lanes] = silu(acc).astype(BF16)

    def conv_head(src, halo, w_ref, b_ref, lanes):
        top = jnp.where(me > 0, halo[:, lanes].astype(F32), 0.0)
        v = jnp.concatenate([top, src[0:16, lanes].astype(F32)], axis=0)
        acc = b_ref[:, lanes] + w_ref[3:4, lanes] * v
        for k in range(1, 4):
            acc = acc + w_ref[3 - k : 4 - k, lanes] * pltpu.roll(v, k, axis=0)
        return silu(acc[8:24]).astype(BF16)

    def stage_main(k):
        xin[k].wait()

        @pl.loop(0, ch // 256)
        def _(j):
            conv_main(xv, xc, wx_ref, bx_ref, pl.ds(pl.multiple_of(k * ch + j * 256, 256), 256))

    def stage_head(k):
        lanes = lanes_of(k)
        xc[0:16, lanes] = conv_head(xv, halo_x, wx_ref, bx_ref, lanes)

    whole = pl.ds(0, 2 * N)
    make_ex(0)
    for cp in small_in[3:]:
        cp.wait()
    stage_main(0)
    conv_main(bc_ref, bcs, wbc_ref, bbc_ref, whole)
    for cp in hal:
        cp.wait_recv()
    bcs[0:16, :] = conv_head(bc_ref, halo_bc, wbc_ref, bbc_ref, whole)
    bt[...] = jnp.transpose(bcs[:, 0:N].astype(F32)).astype(BF16)

    first = c == 0

    def stage_decay_l():
        lcopy.wait_recv()
        own = lo_b[...]
        other = lp_b[...]
        l0 = jnp.where(first, own, other)
        l1 = jnp.where(first, other, own)
        cl = l0 + l1
        cl_b[...] = cl
        xd_b[x] = cl
        for d, xp in enumerate(xpeer):
            rcopy(cl_b, xd_b.at[x], sx_s.at[d], sx_r.at[x], at(z, xp, c)).start()
        dl[...] = dot(pair(jnp.concatenate([jnp.exp2(l0), jnp.exp2(l1)], axis=0)), ex[...])

    oh = pl.multiple_of(c * hr, hr)
    ph = pl.multiple_of((1 - c) * hr, hr)

    def d_copy(k):
        return rcopy(
            sbf.at[pl.ds(ph, hr), lanes_of(k)], srecv.at[:, lanes_of(k)], d_s.at[k], d_r.at[k], partner
        )

    def stage_a(k):
        for j in range(ch // 256):
            lanes = pl.ds(k * ch + j * 256, 256)
            f1e = dot(f1s[...], ex[:, lanes])
            weighted = (xc[:, lanes].astype(F32) * f1e).astype(BF16)
            sbf[:, lanes] = dot(bt[...], weighted).astype(BF16)
        d_copy(k).start()

    def x_copy(k, d):
        xp = xpeer[d]
        rows = pl.ds(pl.multiple_of(xp * xr, xr), xr)
        return rcopy(
            csb.at[rows, lanes_of(k)],
            xrecv.at[x, :, lanes_of(k)],
            x_s.at[k, d],
            x_r.at[k, x],
            at(z, xp, c),
        )

    def x_wait(k, d):
        xp = xpeer[d]
        rcopy(
            csb.at[pl.ds(0, xr), lanes_of(k)],
            xrecv.at[xp, :, lanes_of(k)],
            x_s.at[k, d],
            x_r.at[k, xp],
            at(z, xp, c),
        ).wait_recv()

    def stage_b(k):
        d_copy(k).wait_recv()
        lanes = lanes_of(k)
        mine = sbf[pl.ds(oh, hr), lanes].astype(F32)
        got = srecv[:, lanes].astype(F32)
        e1 = dl[8:9, lanes]
        wm = jnp.where(first, e1, 1.0)
        wg = jnp.where(first, 1.0, e1)
        csb[:, lanes] = (wm * mine + wg * got).astype(BF16)
        for d in range(nx - 1):
            x_copy(k, d).start()
        xrecv[x, :, lanes] = csb[pl.ds(pl.multiple_of(x * xr, xr), xr), lanes]

    def stage_decay_x():
        for d, xp in enumerate(xpeer):
            rcopy(cl_b, xd_b.at[xp], sx_s.at[d], sx_r.at[xp], at(z, xp, c)).wait_recv()
        rows = [xd_b[i][0:1] for i in range(nx)]
        total = rows[0]
        for i in range(1, nx):
            total = total + rows[i]
        after = []
        run = jnp.zeros_like(rows[0])
        for i in reversed(range(nx)):
            after.insert(0, run)
            run = run + rows[i]
        full = jnp.concatenate(
            after + rows + [jnp.zeros_like(rows[0])] * (16 - 2 * nx), axis=0
        )
        dx[...] = dot(pair(jnp.exp2(full)), ex[...])
        pl_b[...] = jnp.broadcast_to(total, (8, 2 * HL))
        zd_b[z] = jnp.broadcast_to(total, (8, 2 * HL))
        for d, zp in enumerate(zpeer):
            rcopy(pl_b, zd_b.at[z], sz_s.at[d], sz_r.at[z], at(zp, x, c)).start()

    def stage_decay_z():
        for d, zp in enumerate(zpeer):
            rcopy(pl_b, zd_b.at[zp], sz_s.at[d], sz_r.at[zp], at(zp, x, c)).wait_recv()
        full = jnp.concatenate(
            [zd_b[i][0:1] for i in range(nz)] + [jnp.zeros((16 - nz, 2 * HL), F32)], axis=0
        )
        full = pair(jnp.exp2(full))
        for k in range(nk):
            lanes = pl.ds(pl.multiple_of(k * ch + z * zw, zw), zw)
            dz[:, k * zw : (k + 1) * zw] = dot(full, ex[:, lanes])

    def z_copy(k, d):
        zp = zpeer[d]
        src = ptb.at[:, pl.ds(pl.multiple_of(k * ch + zp * zw, zw), zw)]
        return rcopy(
            src, zrecv.at[z, :, pl.ds(k * zw, zw)], z_s.at[k, d], z_r.at[k, z], at(zp, x, c)
        )

    def stage_c(k):
        for d in range(nx - 1):
            x_wait(k, d)
        lanes = lanes_of(k)
        tot = dx[0:1, lanes] * xrecv[0, :, lanes].astype(F32)
        for i in range(1, nx):
            tot = tot + dx[i : i + 1, lanes] * xrecv[i, :, lanes].astype(F32)
        ptb[:, lanes] = tot.astype(BF16)
        for d in range(nz - 1):
            z_copy(k, d).start()
        zrecv[z, :, pl.ds(k * zw, zw)] = ptb[:, pl.ds(pl.multiple_of(k * ch + z * zw, zw), zw)]

    def zb_copy(k, d):
        zp = zpeer[d]
        lanes = pl.ds(pl.multiple_of(k * ch + z * zw, zw), zw)
        return rcopy(
            pesend.at[zp, :, pl.ds(k * zw, zw)],
            perecv.at[:, lanes],
            zb_s.at[k, d],
            zb_r.at[k, z],
            at(zp, x, c),
        )

    def stage_d(k):
        own_lanes = pl.ds(k * zw, zw)
        for d, zp in enumerate(zpeer):
            rcopy(
                ptb.at[:, pl.ds(0, zw)],
                zrecv.at[zp, :, own_lanes],
                z_s.at[k, d],
                z_r.at[k, zp],
                at(zp, x, c),
            ).wait_recv()
        state = jnp.zeros((xr, zw), F32)
        for i in range(nz):
            pesend[i, :, own_lanes] = state.astype(BF16)
            state = dz[i : i + 1, own_lanes] * state + zrecv[i, :, own_lanes].astype(F32)
        for d in range(nz - 1):
            zb_copy(k, d).start()
        perecv[:, pl.ds(pl.multiple_of(k * ch + z * zw, zw), zw)] = pesend[z, :, own_lanes]

    def xb_copy(k, d):
        xp = xpeer[d]
        rows = pl.ds(pl.multiple_of(x * xr, xr), xr)
        return rcopy(
            esend.at[xp, :, lanes_of(k)],
            erecv.at[rows, lanes_of(k)],
            xb_s.at[k, d],
            xb_r.at[k, x],
            at(z, xp, c),
        )

    def stage_e(k):
        for d, zp in enumerate(zpeer):
            lanes = pl.ds(pl.multiple_of(k * ch + zp * zw, zw), zw)
            rcopy(
                pesend.at[zp, :, pl.ds(k * zw, zw)],
                perecv.at[:, lanes],
                zb_s.at[k, d],
                zb_r.at[k, zp],
                at(zp, x, c),
            ).wait_recv()
        lanes = lanes_of(k)
        state = perecv[:, lanes].astype(F32)
        for i in range(nx):
            esend[i, :, lanes] = state.astype(BF16)
            if i < nx - 1:
                state = dx[nx + i : nx + i + 1, lanes] * state + xrecv[i, :, lanes].astype(F32)
        for d in range(nx - 1):
            xb_copy(k, d).start()
        erecv[pl.ds(pl.multiple_of(x * xr, xr), xr), lanes] = esend[x, :, lanes]

    def db_copy(k):
        return rcopy(
            entsend.at[:, lanes_of(k)],
            ent.at[pl.ds(oh, hr), lanes_of(k)],
            db_s.at[k],
            db_r.at[k],
            partner,
        )

    def stage_f(k):
        lanes = lanes_of(k)
        for d, xp in enumerate(xpeer):
            rows = pl.ds(pl.multiple_of(xp * xr, xr), xr)
            rcopy(
                esend.at[xp, :, lanes],
                erecv.at[rows, lanes],
                xb_s.at[k, d],
                xb_r.at[k, xp],
                at(z, xp, c),
            ).wait_recv()
        e0 = erecv[:, lanes]
        mine = sbf[pl.ds(oh, hr), lanes]
        got = srecv[:, lanes]
        s0 = jnp.where(first, mine, got).astype(F32)
        e1 = (dl[0:1, lanes] * e0.astype(F32) + s0).astype(BF16)
        entsend[:, lanes] = jnp.where(first, e1, e0)
        db_copy(k).start()
        ent[pl.ds(oh, hr), lanes] = jnp.where(first, e0, e1)

    def prepare():
        cm[...] = bcs[:, N : 2 * N]
        base = ldg[0]
        for g in range(1, ngroup):
            ldg[g] = pltpu.roll(base, 128 - 8 * g, axis=1)
        rt[...] = jnp.transpose(r2s[...])
        f2s[...] = pair(jnp.exp2(base))
        skipd = twice(skip_ref)
        skw[...] = dot(pair(jnp.concatenate([skipd, skipd], 0)), ex[...])[0:8]
        s = lax.dot_general(
            cm[...], bcs[:, 0:N], (((1,), (1,)), ((), ())), preferred_element_type=F32
        )
        low_mask = lax.broadcasted_iota(jnp.int32, (T, T), 0) >= lax.broadcasted_iota(
            jnp.int32, (T, T), 1
        )
        sc[...] = jnp.where(low_mask, s, 0.0)

    hb = T // 2

    def mix_group(g):
        ldt = ldg[g]
        rtile = rt[pl.ds(pl.multiple_of(g * 8, 8), 8), :]
        for j in range(4):
            lanes = pl.ds(pl.multiple_of(g * 512 + j * 128, 128), 128)
            xp = xc[:, lanes]
            lane = lax.broadcasted_iota(jnp.int32, (T, 128), 1)
            xa = jnp.where(lane < 64, xp.astype(F32), 0.0).astype(BF16)
            xb = jnp.where(lane >= 64, xp.astype(F32), 0.0).astype(BF16)
            tops = []
            bots = []
            for a in range(2):
                i = 2 * j + a
                col = ldt[:, i : i + 1]
                row = rtile[i : i + 1, :]
                tl = jnp.exp2(jnp.minimum(col[0:hb] - row[:, 0:hb], 126.0)) * sc[0:hb, 0:hb]
                bl = jnp.exp2(col[hb:T] - row[:, 0:hb]) * sc[hb:T, 0:hb]
                br = jnp.exp2(jnp.minimum(col[hb:T] - row[:, hb:T], 126.0)) * sc[hb:T, hb:T]
                tops.append(tl.astype(BF16))
                bots += [bl.astype(BF16), br.astype(BF16)]
            yt = dot(jnp.concatenate(tops, 1), jnp.concatenate([xa[0:hb], xb[0:hb]], 0))
            yb = dot(jnp.concatenate(bots, 1), jnp.concatenate([xa, xb], 0))
            sk = skw[0:1, lanes] * xp.astype(F32)
            inside[0:hb, lanes] = yt + sk[0:hb]
            inside[hb:T, lanes] = yb + sk[hb:T]

    def silu_group(g):
        lanes = pl.ds(g * 512, 512)
        zs[:, lanes] = silu(zv[:, lanes].astype(F32))

    def stage_g(k):
        db_copy(k).wait_recv()

        @pl.loop(0, ch // 256)
        def _(j):
            lanes = pl.ds(pl.multiple_of(k * ch + j * 256, 256), 256)
            f2e = dot(f2s[...], ex[:, lanes])
            y = (inside[:, lanes] + f2e * dot(cm[...], ent[:, lanes])).astype(BF16)
            gated = y.astype(F32) * zs[:, lanes]
            inside[:, lanes] = gated
            sq = gated * gated
            ssq[...] += sq[:, 0:128] + sq[:, 128:256]

    fill = [functools.partial(mix_group, g) for g in range(ngroup)]
    fill += [functools.partial(silu_group, g) for g in range(ngroup)]

    def filler(n):
        for _ in range(n):
            if fill:
                fill.pop(0)()

    stage_head(0)
    stage_a(0)
    for k in range(1, nk):
        make_ex(k)
    stage_main(1)
    stage_head(1)
    stage_a(1)
    stage_decay_l()
    stage_b(0)
    for k in range(2, nk):
        stage_main(k)
        stage_head(k)
        stage_a(k)
        stage_b(k - 1)
    stage_decay_x()
    stage_b(nk - 1)
    prepare()
    ssq[...] = jnp.zeros_like(ssq)
    zin.wait()

    for s in range(nk):
        stage_c(s)
        filler(1)
    filler(1)
    stage_decay_z()
    for s in range(nk):
        stage_d(s)
        filler(1)
    filler(3)
    for s in range(nk):
        stage_e(s)
        filler(1)
    while fill:
        filler(1)
    stage_f(0)
    for s in range(1, nk):
        stage_f(s)
        stage_g(s - 1)
    stage_g(nk - 1)

    ms = jnp.sum(ssq[...], axis=1, keepdims=True) * (1.0 / di)
    rs = lax.rsqrt(ms + 1e-05)
    outs = []
    for i in range(nk):

        @pl.loop(0, ch // 256)
        def _(j):
            lanes = pl.ds(pl.multiple_of(i * ch + j * 256, 256), 256)
            ov[:, lanes] = (inside[:, lanes] * rs * gain_ref[:, lanes]).astype(BF16)

        cp = pltpu.make_async_copy(ov.at[:, lanes_of(i)], out_hbm.at[:, lanes_of(i)], sem_out.at[i])
        cp.start()
        outs.append(cp)

    for cp in hal:
        cp.wait_send()
    lcopy.wait_send()
    for d, xp in enumerate(xpeer):
        rcopy(cl_b, xd_b.at[x], sx_s.at[d], sx_r.at[x], at(z, xp, c)).wait_send()
    for d, zp in enumerate(zpeer):
        rcopy(pl_b, zd_b.at[z], sz_s.at[d], sz_r.at[z], at(zp, x, c)).wait_send()
    for k in range(nk):
        d_copy(k).wait_send()
        db_copy(k).wait_send()
        for d in range(nx - 1):
            x_copy(k, d).wait_send()
            xb_copy(k, d).wait_send()
        for d in range(nz - 1):
            z_copy(k, d).wait_send()
            zb_copy(k, d).wait_send()
    for cp in outs:
        cp.wait()


def make_body(nz, nx, nk):
    def body(x_raw, z_gate, bc_raw, dt_raw, wx, bx, wbc, bbc, dtb, alog, skip, gain):
        di = x_raw.shape[1]
        ch = di // nk
        zw = ch // nz
        hr = N // 2
        xr = hr // nx
        ng = di // 512
        vm = lambda *s: pltpu.VMEM(s, F32)
        vb = lambda *s: pltpu.VMEM(s, BF16)
        dma = lambda *s: pltpu.SemaphoreType.DMA(s)
        anyspec = pl.BlockSpec(memory_space=pl.ANY)
        scratch = [
            vb(T, 2 * N),
            vb(HL, T),
            vm(4, di),
            vm(1, di),
            vm(4, 2 * N),
            vm(1, 2 * N),
            vm(1, HL),
            vm(1, HL),
            vm(1, HL),
            vm(1, di),
            vb(T, 2 * N),
            vm(T, di),
            vb(T, di),
            vb(T, di),
            vb(T, di),
            vb(8, di),
            vb(8, 2 * N),
            vm(T, 128),
            vb(128, di),
            vm(ng, T, 128),
            vm(128, T),
            vb(T, 128),
            vb(T, 128),
            vb(N, T),
            vb(T, N),
            vm(T, T),
            vm(8, di),
            vm(T, di),
            vm(T, 128),
            vb(T, di),
            vm(8, 128),
            vm(8, 128),
            vm(8, 128),
            vm(nx, 8, 128),
            vm(8, 128),
            vm(nz, 8, 128),
            vm(16, di),
            vm(16, di),
            vm(16, nk * zw),
            vb(N, di),
            vb(hr, di),
            vb(hr, di),
            vb(nx, xr, di),
            vb(xr, di),
            vb(nz, xr, nk * zw),
            vb(nz, xr, nk * zw),
            vb(xr, di),
            vb(nx, xr, di),
            vb(hr, di),
            vb(hr, di),
            vb(N, di),
            dma(nk + 1),
            dma(10),
            dma(nk),
            dma(4),
            dma(2),
            dma(nx),
            dma(nx),
            dma(nz),
            dma(nz),
            dma(nk),
            dma(nk),
            dma(nk, nx),
            dma(nk, nx),
            dma(nk, nz),
            dma(nk, nz),
            dma(nk, nz),
            dma(nk, nz),
            dma(nk, nx),
            dma(nk, nx),
            dma(nk),
            dma(nk),
        ]
        return pl.pallas_call(
            functools.partial(kernel, nz, nx, di, nk),
            out_shape=jax.ShapeDtypeStruct((T, di), BF16),
            in_specs=[anyspec] * 12,
            out_specs=anyspec,
            scratch_shapes=scratch,
            compiler_params=pltpu.CompilerParams(
                collective_id=0, has_side_effects=True, vmem_limit_bytes=60 * 1024 * 1024
            ),
        )(
            x_raw,
            z_gate,
            bc_raw,
            dt_raw.T,
            wx,
            bx.reshape(1, -1),
            wbc,
            bbc.reshape(1, -1),
            dtb.reshape(1, -1),
            alog.reshape(1, -1),
            skip.reshape(1, -1),
            gain.reshape(1, -1),
        )

    return body


def solution(mesh):
    nx = 4
    nz = mesh.shape["seq"] // (2 * nx)
    tok = P(("vol", "seq"), None)
    return jax.shard_map(
        make_body(nz, nx, 4),
        mesh=mesh,
        in_specs=(tok, tok, tok, tok) + (P(),) * 8,
        out_specs=tok,
        check_vma=False,
    )
```

```python
import functools

import jax
import jax.numpy as jnp
from jax import lax
from jax.experimental import pallas as pl
from jax.experimental.pallas import tpu as pltpu
from jax.sharding import PartitionSpec as P

T = 256
N = 128
HL = 64
LOG2E = 1.4426950408889634
F32 = jnp.float32
BF16 = jnp.bfloat16


def dot(a, b):
    return jnp.dot(a, b, preferred_element_type=F32)


def silu(v):
    return v / (1.0 + jnp.exp(-v))


def kernel(
    nz,
    nx,
    di,
    nk,
    no,
    x_hbm,
    z_hbm,
    bc_hbm,
    dt_hbm,
    wx_hbm,
    bx_hbm,
    wbc_hbm,
    bbc_hbm,
    dtb_hbm,
    alog_hbm,
    skip_hbm,
    inside,
    rs_ref,
    bc_ref,
    dt_ref,
    wx_ref,
    bx_ref,
    wbc_ref,
    bbc_ref,
    dtb_ref,
    alog_ref,
    skip_ref,
    bcs,
    zs,
    xv,
    zv,
    xc,
    halo_x,
    halo_bc,
    r2s,
    ex,
    ldg,
    rt,
    f1s,
    f2s,
    bt,
    cm,
    sc,
    skw,
    ssq,
    lo_b,
    lp_b,
    cl_b,
    xd_b,
    pl_b,
    zd_b,
    dx,
    dl,
    dz,
    sbf,
    srecv,
    csb,
    xrecv,
    ptb,
    zrecv,
    pesend,
    perecv,
    esend,
    erecv,
    entsend,
    ent,
    sem_in,
    sem_small,
    sem_halo,
    sem_l,
    sx_s,
    sx_r,
    sz_s,
    sz_r,
    d_s,
    d_r,
    x_s,
    x_r,
    z_s,
    z_r,
    zb_s,
    zb_r,
    xb_s,
    xb_r,
    db_s,
    db_r,
):
    ch = di // nk
    zw = ch // no
    hr = N // 2
    xr = hr // nx
    ngroup = di // 512

    me = lax.axis_index("seq")
    c = lax.rem(me, 2)
    x = lax.rem(me // 2, nx)
    z = me // (2 * nx)
    nseq = 2 * nx * nz

    def at(zz, xx, cc):
        return (zz * nx + xx) * 2 + cc

    partner = at(z, x, 1 - c)
    nxt = lax.rem(me + 1, nseq)
    prv = lax.rem(me + nseq - 1, nseq)
    xpeer = [lax.rem(x + d, nx) for d in range(1, nx)]
    zpeer = [lax.rem(z + d, nz) for d in range(1, nz)]

    barrier = pltpu.get_barrier_semaphore()
    peers = [partner, nxt, prv]
    peers += [at(z, xp, c) for xp in xpeer]
    peers += [at(zp, x, c) for zp in zpeer]
    for p in peers:
        pl.semaphore_signal(barrier, inc=1, device_id={"seq": p})

    def rcopy(src, dst, ss, rs, dev):
        return pltpu.make_async_remote_copy(
            src_ref=src, dst_ref=dst, send_sem=ss, recv_sem=rs, device_id={"seq": dev}
        )

    def lanes_of(k):
        return pl.ds(k * ch, ch)

    smalls = [
        (dt_hbm, dt_ref),
        (dtb_hbm, dtb_ref),
        (alog_hbm, alog_ref),
        (bc_hbm, bc_ref),
        (wx_hbm, wx_ref),
        (bx_hbm, bx_ref),
        (wbc_hbm, wbc_ref),
        (bbc_hbm, bbc_ref),
        (skip_hbm, skip_ref),
    ]
    small_in = [pltpu.make_async_copy(p, q, sem_small.at[i]) for i, (p, q) in enumerate(smalls)]
    xin = [
        pltpu.make_async_copy(x_hbm.at[:, lanes_of(k)], xv.at[:, lanes_of(k)], sem_in.at[k])
        for k in range(nk)
    ]
    zin = pltpu.make_async_copy(z_hbm, zv, sem_in.at[nk])
    for cp in small_in[0:3]:
        cp.start()
    xin[0].start()
    for cp in small_in[3:]:
        cp.start()
    for cp in xin[1:]:
        cp.start()
    zin.start()

    def twice(ref):
        row = jnp.broadcast_to(ref[...], (8, HL))
        return jnp.concatenate([row, row], axis=1)

    for cp in small_in[0:3]:
        cp.wait()
    dtv = dt_ref[...].astype(F32)
    raw = jnp.transpose(jnp.concatenate([dtv, dtv], axis=0)) + twice(dtb_ref)[0:1]
    step = jnp.maximum(raw, 0.0) + jnp.log1p(jnp.exp(-jnp.abs(raw)))
    rate = -jnp.exp(twice(alog_ref)[0:1]) * step
    low = lax.broadcasted_iota(jnp.int32, (T, T), 0) >= lax.broadcasted_iota(jnp.int32, (T, T), 1)
    ld2 = jnp.dot(
        jnp.where(low, 1.0, 0.0),
        rate,
        precision=lax.Precision.HIGHEST,
        preferred_element_type=F32,
    ) * LOG2E
    r2 = ld2 - jnp.log(step) * LOG2E
    last2 = ld2[T - 1 : T, :]
    ldg[0] = ld2
    r2s[...] = r2

    def pair(v):
        hi = v.astype(BF16).astype(F32)
        lane = lax.broadcasted_iota(jnp.int32, v.shape, 1)
        return jnp.where(lane < HL, hi, v - hi).astype(BF16)

    f1s[...] = pair(jnp.exp2(last2 - r2))
    lo_b[...] = jnp.broadcast_to(last2, (8, 2 * HL))

    def make_ex(k):
        @pl.loop(0, ch // 256)
        def _(j):
            base = k * ch + j * 256
            row = lax.broadcasted_iota(jnp.int32, (128, 256), 0) & 63
            head = (lax.broadcasted_iota(jnp.int32, (128, 256), 1) + base) >> 6
            ex[:, pl.ds(pl.multiple_of(base, 256), 256)] = jnp.where(row == head, 1.0, 0.0).astype(BF16)

    pl.semaphore_wait(barrier, len(peers))
    hal = [
        rcopy(x_hbm.at[pl.ds(T - 8, 8), :], halo_x, sem_halo.at[0], sem_halo.at[1], nxt),
        rcopy(bc_hbm.at[pl.ds(T - 8, 8), :], halo_bc, sem_halo.at[2], sem_halo.at[3], nxt),
    ]
    for cp in hal:
        cp.start()
    lcopy = rcopy(lo_b, lp_b, sem_l.at[0], sem_l.at[1], partner)
    lcopy.start()

    def conv_main(src, dst, w_ref, b_ref, lanes):
        v = src[:, lanes].astype(F32)
        acc = b_ref[:, lanes] + w_ref[3:4, lanes] * v
        for k in range(1, 4):
            acc = acc + w_ref[3 - k : 4 - k, lanes] * pltpu.roll(v, k, axis=0)
        dst[:, lanes] = silu(acc).astype(BF16)

    def conv_head(src, halo, w_ref, b_ref, lanes):
        top = jnp.where(me > 0, halo[:, lanes].astype(F32), 0.0)
        v = jnp.concatenate([top, src[0:16, lanes].astype(F32)], axis=0)
        acc = b_ref[:, lanes] + w_ref[3:4, lanes] * v
        for k in range(1, 4):
            acc = acc + w_ref[3 - k : 4 - k, lanes] * pltpu.roll(v, k, axis=0)
        return silu(acc[8:24]).astype(BF16)

    def stage_main(k):
        xin[k].wait()

        @pl.loop(0, ch // 256)
        def _(j):
            conv_main(xv, xc, wx_ref, bx_ref, pl.ds(pl.multiple_of(k * ch + j * 256, 256), 256))

    def stage_head(k):
        lanes = lanes_of(k)
        xc[0:16, lanes] = conv_head(xv, halo_x, wx_ref, bx_ref, lanes)

    whole = pl.ds(0, 2 * N)
    make_ex(0)
    for cp in small_in[3:]:
        cp.wait()
    stage_main(0)
    conv_main(bc_ref, bcs, wbc_ref, bbc_ref, whole)
    make_ex(1)
    stage_main(1)
    stage_main(2 % nk) if nk > 2 else None

    @pl.when(z == 0)
    def _():
        perecv[...] = jnp.zeros_like(perecv)

    for cp in hal:
        cp.wait_recv()
    bcs[0:16, :] = conv_head(bc_ref, halo_bc, wbc_ref, bbc_ref, whole)
    bt[...] = jnp.transpose(bcs[:, 0:N].astype(F32)).astype(BF16)

    first = c == 0

    def stage_decay_l():
        lcopy.wait_recv()
        own = lo_b[...]
        other = lp_b[...]
        l0 = jnp.where(first, own, other)
        l1 = jnp.where(first, other, own)
        cl = l0 + l1
        cl_b[...] = cl
        xd_b[x] = cl
        for d, xp in enumerate(xpeer):
            rcopy(cl_b, xd_b.at[x], sx_s.at[d], sx_r.at[x], at(z, xp, c)).start()
        dl[...] = dot(pair(jnp.concatenate([jnp.exp2(l0), jnp.exp2(l1)], axis=0)), ex[...])

    oh = pl.multiple_of(c * hr, hr)
    ph = pl.multiple_of((1 - c) * hr, hr)

    def d_copy(k):
        return rcopy(
            sbf.at[pl.ds(ph, hr), lanes_of(k)], srecv.at[:, lanes_of(k)], d_s.at[k], d_r.at[k], partner
        )

    def stage_a(k):
        for j in range(ch // 256):
            lanes = pl.ds(k * ch + j * 256, 256)
            f1e = dot(f1s[...], ex[:, lanes])
            weighted = (xc[:, lanes].astype(F32) * f1e).astype(BF16)
            sbf[:, lanes] = dot(bt[...], weighted).astype(BF16)
        d_copy(k).start()

    def x_copy(k, d):
        xp = xpeer[d]
        rows = pl.ds(pl.multiple_of(xp * xr, xr), xr)
        return rcopy(
            csb.at[rows, lanes_of(k)],
            xrecv.at[x, :, lanes_of(k)],
            x_s.at[k, d],
            x_r.at[k, x],
            at(z, xp, c),
        )

    def x_wait(k, d):
        xp = xpeer[d]
        rcopy(
            csb.at[pl.ds(0, xr), lanes_of(k)],
            xrecv.at[xp, :, lanes_of(k)],
            x_s.at[k, d],
            x_r.at[k, xp],
            at(z, xp, c),
        ).wait_recv()

    def stage_b(k):
        d_copy(k).wait_recv()
        lanes = lanes_of(k)
        mine = sbf[pl.ds(oh, hr), lanes].astype(F32)
        got = srecv[:, lanes].astype(F32)
        e1 = dl[8:9, lanes]
        wm = jnp.where(first, e1, 1.0)
        wg = jnp.where(first, 1.0, e1)
        csb[:, lanes] = (wm * mine + wg * got).astype(BF16)
        for d in range(nx - 1):
            x_copy(k, d).start()
        xrecv[x, :, lanes] = csb[pl.ds(pl.multiple_of(x * xr, xr), xr), lanes]

    def zd_copy(o):
        return rcopy(pl_b, zd_b.at[z], sz_s.at[o], sz_r.at[z], at(o, x, c))

    def stage_decay_x():
        for d, xp in enumerate(xpeer):
            rcopy(cl_b, xd_b.at[xp], sx_s.at[d], sx_r.at[xp], at(z, xp, c)).wait_recv()
        rows = [xd_b[i][0:1] for i in range(nx)]
        total = rows[0]
        for i in range(1, nx):
            total = total + rows[i]
        after = []
        run = jnp.zeros_like(rows[0])
        for i in reversed(range(nx)):
            after.insert(0, run)
            run = run + rows[i]
        full = jnp.concatenate(
            after + rows + [jnp.zeros_like(rows[0])] * (16 - 2 * nx), axis=0
        )
        dx[...] = dot(pair(jnp.exp2(full)), ex[...])
        pl_b[...] = jnp.broadcast_to(total, (8, 2 * HL))
        for o in range(no):

            @pl.when(z == o)
            def _():
                zd_b[o] = jnp.broadcast_to(total, (8, 2 * HL))

            @pl.when((z != o) & (z < nz - 1))
            def _():
                zd_copy(o).start()

    def own_lanes(k):
        return pl.ds(k * zw, zw)

    def lanes_to(k, o):
        return pl.ds(k * ch + o * zw, zw)

    def z_copy(k, o):
        return rcopy(
            ptb.at[:, lanes_to(k, o)],
            zrecv.at[z, :, own_lanes(k)],
            z_s.at[k, o],
            z_r.at[k, z],
            at(o, x, c),
        )

    def stage_c(k):
        for d in range(nx - 1):
            x_wait(k, d)
        lanes = lanes_of(k)
        tot = dx[0:1, lanes] * xrecv[0, :, lanes].astype(F32)
        for i in range(1, nx):
            tot = tot + dx[i : i + 1, lanes] * xrecv[i, :, lanes].astype(F32)
        ptb[:, lanes] = tot.astype(BF16)
        for o in range(no):

            @pl.when(z == o)
            def _():
                zrecv[o, :, own_lanes(k)] = ptb[:, lanes_to(k, o)]

            @pl.when((z != o) & (z < nz - 1))
            def _():
                z_copy(k, o).start()

    def zb_copy(k, o, j):
        return rcopy(
            pesend.at[j, :, own_lanes(k)],
            perecv.at[:, lanes_to(k, o)],
            zb_s.at[k, j],
            zb_r.at[k, o],
            at(j, x, c),
        )

    def stage_d():
        lead = [0.0, 1.5, 2.7, 3.5, 4.3, 4.6, 4.8, 5.0]
        order = sorted(
            (lead[min(i, 7)] + 1.1 * k, i, k) for i in range(nz - 1) for k in range(nk)
        )
        for o in range(no):

            @pl.when(z == o)
            def _():
                states = [jnp.zeros((xr, zw), F32) for _ in range(nk)]
                seen = []
                for _, i, k in order:
                    if i not in seen:
                        seen.append(i)
                        if i != o:
                            rcopy(pl_b, zd_b.at[i], sz_s.at[0], sz_r.at[i], at(i, x, c)).wait_recv()
                        e = jnp.exp2(zd_b[i])
                        full = pair(jnp.concatenate([e, e], axis=0))
                        for q in range(nk):
                            dz[i, :, q * zw : (q + 1) * zw] = dot(full, ex[:, lanes_to(q, o)])
                    if i != o:
                        rcopy(
                            ptb.at[:, pl.ds(0, zw)],
                            zrecv.at[i, :, own_lanes(k)],
                            z_s.at[k, 0],
                            z_r.at[k, i],
                            at(i, x, c),
                        ).wait_recv()
                    old = states[k]
                    new = dz[i, 0:1, own_lanes(k)] * old + zrecv[i, :, own_lanes(k)].astype(F32)
                    states[k] = new
                    if i + 1 == o:
                        perecv[:, lanes_to(k, o)] = new.astype(BF16)
                    else:
                        pesend[i + 1, :, own_lanes(k)] = new.astype(BF16)
                        zb_copy(k, o, i + 1).start()

    def xb_copy(k, d):
        xp = xpeer[d]
        rows = pl.ds(pl.multiple_of(x * xr, xr), xr)
        return rcopy(
            esend.at[xp, :, lanes_of(k)],
            erecv.at[rows, lanes_of(k)],
            xb_s.at[k, d],
            xb_r.at[k, x],
            at(z, xp, c),
        )

    def stage_e(k):
        for o in range(no):

            @pl.when((z != o) & (z > 0))
            def _():
                rcopy(
                    pesend.at[0, :, own_lanes(k)],
                    perecv.at[:, lanes_to(k, o)],
                    zb_s.at[k, 0],
                    zb_r.at[k, o],
                    at(o, x, c),
                ).wait_recv()

        lanes = lanes_of(k)
        state = perecv[:, lanes].astype(F32)
        for i in range(nx):
            esend[i, :, lanes] = state.astype(BF16)
            if i < nx - 1:
                state = dx[nx + i : nx + i + 1, lanes] * state + xrecv[i, :, lanes].astype(F32)
        for d in range(nx - 1):
            xb_copy(k, d).start()
        erecv[pl.ds(pl.multiple_of(x * xr, xr), xr), lanes] = esend[x, :, lanes]

    def db_copy(k):
        return rcopy(
            entsend.at[:, lanes_of(k)],
            ent.at[pl.ds(oh, hr), lanes_of(k)],
            db_s.at[k],
            db_r.at[k],
            partner,
        )

    def stage_f(k):
        lanes = lanes_of(k)
        for d, xp in enumerate(xpeer):
            rows = pl.ds(pl.multiple_of(xp * xr, xr), xr)
            rcopy(
                esend.at[xp, :, lanes],
                erecv.at[rows, lanes],
                xb_s.at[k, d],
                xb_r.at[k, xp],
                at(z, xp, c),
            ).wait_recv()
        e0 = erecv[:, lanes]
        mine = sbf[pl.ds(oh, hr), lanes]
        got = srecv[:, lanes]
        s0 = jnp.where(first, mine, got).astype(F32)
        e1 = (dl[0:1, lanes] * e0.astype(F32) + s0).astype(BF16)
        entsend[:, lanes] = jnp.where(first, e1, e0)
        db_copy(k).start()
        ent[pl.ds(oh, hr), lanes] = jnp.where(first, e0, e1)

    def prepare():
        cm[...] = bcs[:, N : 2 * N]
        base = ldg[0]
        for g in range(1, ngroup):
            ldg[g] = pltpu.roll(base, 128 - 8 * g, axis=1)
        rt[...] = jnp.transpose(r2s[...])
        f2s[...] = pair(jnp.exp2(base))
        skipd = twice(skip_ref)
        skw[...] = dot(pair(jnp.concatenate([skipd, skipd], 0)), ex[...])[0:8]
        s = lax.dot_general(
            cm[...], bcs[:, 0:N], (((1,), (1,)), ((), ())), preferred_element_type=F32
        )
        low_mask = lax.broadcasted_iota(jnp.int32, (T, T), 0) >= lax.broadcasted_iota(
            jnp.int32, (T, T), 1
        )
        sc[...] = jnp.where(low_mask, s, 0.0)

    hb = T // 2

    def mix_group(g):
        ldt = ldg[g]
        rtile = rt[pl.ds(pl.multiple_of(g * 8, 8), 8), :]
        for j in range(4):
            lanes = pl.ds(pl.multiple_of(g * 512 + j * 128, 128), 128)
            xp = xc[:, lanes]
            lane = lax.broadcasted_iota(jnp.int32, (T, 128), 1)
            xa = jnp.where(lane < 64, xp.astype(F32), 0.0).astype(BF16)
            xb = jnp.where(lane >= 64, xp.astype(F32), 0.0).astype(BF16)
            tops = []
            bots = []
            for a in range(2):
                i = 2 * j + a
                col = ldt[:, i : i + 1]
                row = rtile[i : i + 1, :]
                tl = jnp.exp2(jnp.minimum(col[0:hb] - row[:, 0:hb], 126.0)) * sc[0:hb, 0:hb]
                bl = jnp.exp2(col[hb:T] - row[:, 0:hb]) * sc[hb:T, 0:hb]
                br = jnp.exp2(jnp.minimum(col[hb:T] - row[:, hb:T], 126.0)) * sc[hb:T, hb:T]
                tops.append(tl.astype(BF16))
                bots += [bl.astype(BF16), br.astype(BF16)]
            yt = dot(jnp.concatenate(tops, 1), jnp.concatenate([xa[0:hb], xb[0:hb]], 0))
            yb = dot(jnp.concatenate(bots, 1), jnp.concatenate([xa, xb], 0))
            sk = skw[0:1, lanes] * xp.astype(F32)
            inside[0:hb, lanes] = yt + sk[0:hb]
            inside[hb:T, lanes] = yb + sk[hb:T]

    def silu_group(g):
        lanes = pl.ds(g * 512, 512)
        zs[:, lanes] = silu(zv[:, lanes].astype(F32))

    def stage_g(k):
        db_copy(k).wait_recv()

        @pl.loop(0, ch // 256)
        def _(j):
            lanes = pl.ds(pl.multiple_of(k * ch + j * 256, 256), 256)
            f2e = dot(f2s[...], ex[:, lanes])
            y = (inside[:, lanes] + f2e * dot(cm[...], ent[:, lanes])).astype(BF16)
            gated = y.astype(F32) * zs[:, lanes]
            inside[:, lanes] = gated
            sq = gated * gated
            ssq[...] += sq[:, 0:128] + sq[:, 128:256]

    fill = [functools.partial(mix_group, g) for g in range(ngroup)]
    fill += [functools.partial(silu_group, g) for g in range(ngroup)]

    def filler(n):
        for _ in range(n):
            if fill:
                fill.pop(0)()

    stage_head(0)
    stage_a(0)
    stage_head(1)
    stage_a(1)
    for k in range(2, nk):
        make_ex(k)
    stage_decay_l()
    stage_b(0)
    for k in range(2, nk):
        if k > 2:
            stage_main(k)
        stage_head(k)
        stage_a(k)
        stage_b(k - 1)
    stage_decay_x()
    stage_b(nk - 1)
    prepare()
    ssq[...] = jnp.zeros_like(ssq)
    zin.wait()

    for s in range(nk):
        stage_c(s)
        filler(1)
    while fill:
        filler(1)
    stage_d()
    for s in range(nk):
        stage_e(s)
    stage_f(0)
    for s in range(1, nk):
        stage_f(s)
        stage_g(s - 1)
    stage_g(nk - 1)

    ms = jnp.sum(ssq[...], axis=1, keepdims=True) * (1.0 / di)
    rs_ref[...] = jnp.broadcast_to(lax.rsqrt(ms + 1e-05), (T, 128))

    for cp in hal:
        cp.wait_send()
    lcopy.wait_send()
    for d, xp in enumerate(xpeer):
        rcopy(cl_b, xd_b.at[x], sx_s.at[d], sx_r.at[x], at(z, xp, c)).wait_send()
    for o in range(no):

        @pl.when((z != o) & (z < nz - 1))
        def _():
            zd_copy(o).wait_send()
            for k in range(nk):
                z_copy(k, o).wait_send()

        @pl.when(z == o)
        def _():
            for k in range(nk):
                for j in range(1, nz):
                    if j != o:
                        zb_copy(k, o, j).wait_send()

    for k in range(nk):
        d_copy(k).wait_send()
        db_copy(k).wait_send()
        for d in range(nx - 1):
            x_copy(k, d).wait_send()
            xb_copy(k, d).wait_send()


def norm_kernel(gated, scale, gain_hbm, out_hbm, ov, gain, sem_in, sem_out):
    di = gated.shape[1]
    quarter = di // 4
    cp = pltpu.make_async_copy(gain_hbm, gain, sem_in.at[0])
    cp.start()
    cp.wait()
    outs = []
    for i in range(4):

        @pl.loop(0, quarter // 128)
        def _(j):
            lanes = pl.ds(pl.multiple_of(i * quarter + j * 128, 128), 128)
            ov[:, lanes] = (gated[:, lanes] * scale[...] * gain[:, lanes]).astype(BF16)

        lanes = pl.ds(i * quarter, quarter)
        out = pltpu.make_async_copy(ov.at[:, lanes], out_hbm.at[:, lanes], sem_out.at[i])
        out.start()
        outs.append(out)
    for out in outs:
        out.wait()


def make_body(nz, nx, nk, no):
    def body(x_raw, z_gate, bc_raw, dt_raw, wx, bx, wbc, bbc, dtb, alog, skip, gain):
        di = x_raw.shape[1]
        ch = di // nk
        zw = ch // no
        hr = N // 2
        xr = hr // nx
        ng = di // 512
        vm = lambda *s: pltpu.VMEM(s, F32)
        vb = lambda *s: pltpu.VMEM(s, BF16)
        dma = lambda *s: pltpu.SemaphoreType.DMA(s)
        anyspec = pl.BlockSpec(memory_space=pltpu.HBM)
        scratch = [
            vb(T, 2 * N),
            vb(HL, T),
            vm(4, di),
            vm(1, di),
            vm(4, 2 * N),
            vm(1, 2 * N),
            vm(1, HL),
            vm(1, HL),
            vm(1, HL),
            vb(T, 2 * N),
            vm(T, di),
            vb(T, di),
            vb(T, di),
            vb(T, di),
            vb(8, di),
            vb(8, 2 * N),
            vm(T, 128),
            vb(128, di),
            vm(ng, T, 128),
            vm(128, T),
            vb(T, 128),
            vb(T, 128),
            vb(N, T),
            vb(T, N),
            vm(T, T),
            vm(8, di),
            vm(T, 128),
            vm(8, 128),
            vm(8, 128),
            vm(8, 128),
            vm(nx, 8, 128),
            vm(8, 128),
            vm(nz, 8, 128),
            vm(16, di),
            vm(16, di),
            vm(nz, 16, nk * zw),
            vb(N, di),
            vb(hr, di),
            vb(hr, di),
            vb(nx, xr, di),
            vb(xr, di),
            vb(nz, xr, nk * zw),
            vb(nz, xr, nk * zw),
            vb(xr, di),
            vb(nx, xr, di),
            vb(hr, di),
            vb(hr, di),
            vb(N, di),
            dma(nk + 1),
            dma(9),
            dma(4),
            dma(2),
            dma(nx),
            dma(nx),
            dma(nz),
            dma(nz),
            dma(nk),
            dma(nk),
            dma(nk, nx),
            dma(nk, nx),
            dma(nk, nz),
            dma(nk, nz),
            dma(nk, nz),
            dma(nk, nz),
            dma(nk, nx),
            dma(nk, nx),
            dma(nk),
            dma(nk),
        ]
        gated, scale = pl.pallas_call(
            functools.partial(kernel, nz, nx, di, nk, no),
            out_shape=(
                pltpu.VMEM((T, di), F32),
                pltpu.VMEM((T, 128), F32),
            ),
            in_specs=[anyspec] * 11,
            out_specs=(pl.BlockSpec(memory_space=pltpu.VMEM),) * 2,
            scratch_shapes=scratch,
            compiler_params=pltpu.CompilerParams(
                collective_id=0, has_side_effects=True, vmem_limit_bytes=48 * 1024 * 1024
            ),
        )(
            *(
                pltpu.with_memory_space_constraint(a, pltpu.HBM)
                for a in (
            x_raw,
            z_gate,
            bc_raw,
            dt_raw.T,
            wx,
            bx.reshape(1, -1),
            wbc,
            bbc.reshape(1, -1),
            dtb.reshape(1, -1),
            alog.reshape(1, -1),
            skip.reshape(1, -1),
                )
            )
        )
        full = pl.BlockSpec(memory_space=pltpu.VMEM)
        return pl.pallas_call(
            norm_kernel,
            out_shape=jax.ShapeDtypeStruct((T, di), BF16),
            in_specs=[full, full, anyspec],
            out_specs=anyspec,
            scratch_shapes=[vb(T, di), vm(1, di), dma(1), dma(4)],
            compiler_params=pltpu.CompilerParams(vmem_limit_bytes=16 * 1024 * 1024),
        )(gated, scale, pltpu.with_memory_space_constraint(gain.reshape(1, -1), pltpu.HBM))

    return body


def solution(mesh):
    nx = 4
    nz = mesh.shape["seq"] // (2 * nx)
    tok = P(("vol", "seq"), None)
    return jax.shard_map(
        make_body(nz, nx, 4, 2),
        mesh=mesh,
        in_specs=(tok, tok, tok, tok) + (P(),) * 8,
        out_specs=tok,
        check_vma=False,
    )
```

```python
import functools

import jax
import jax.numpy as jnp
from jax import lax
from jax.experimental import pallas as pl
from jax.experimental.pallas import tpu as pltpu
from jax.sharding import PartitionSpec as P

T = 256
N = 128
HL = 64
LOG2E = 1.4426950408889634
F32 = jnp.float32
BF16 = jnp.bfloat16


def dot(a, b):
    return jnp.dot(a, b, preferred_element_type=F32)


def silu(v):
    return v / (1.0 + jnp.exp(-v))


def kernel(
    nz,
    nx,
    di,
    nk,
    no,
    x_hbm,
    z_hbm,
    bc_hbm,
    dt_hbm,
    wx_hbm,
    bx_hbm,
    wbc_hbm,
    bbc_hbm,
    dtb_hbm,
    alog_hbm,
    skip_hbm,
    inside,
    rs_ref,
    bc_ref,
    dt_ref,
    wx_ref,
    bx_ref,
    wbc_ref,
    bbc_ref,
    dtb_ref,
    alog_ref,
    skip_ref,
    bcs,
    zs,
    xv,
    zv,
    xc,
    halo_x,
    halo_bc,
    r2s,
    ex,
    ldg,
    rt,
    f1s,
    f2s,
    bt,
    cm,
    sc,
    skw,
    ssq,
    lo_b,
    lp_b,
    cl_b,
    xd_b,
    pl_b,
    zd_b,
    dx,
    dl,
    dz,
    sbf,
    srecv,
    csb,
    xrecv,
    ptb,
    zrecv,
    pesend,
    perecv,
    esend,
    erecv,
    entsend,
    ent,
    sem_in,
    sem_small,
    sem_halo,
    sem_l,
    sx_s,
    sx_r,
    sz_s,
    sz_r,
    d_s,
    d_r,
    x_s,
    x_r,
    z_s,
    z_r,
    zb_s,
    zb_r,
    xb_s,
    xb_r,
    db_s,
    db_r,
):
    ch = di // nk
    zw = ch // no
    hr = N // 2
    xr = hr // nx
    ngroup = di // 512

    me = lax.axis_index("seq")
    c = lax.rem(me, 2)
    x = lax.rem(me // 2, nx)
    z = me // (2 * nx)
    nseq = 2 * nx * nz

    def at(zz, xx, cc):
        return (zz * nx + xx) * 2 + cc

    partner = at(z, x, 1 - c)
    nxt = lax.rem(me + 1, nseq)
    prv = lax.rem(me + nseq - 1, nseq)
    xpeer = [lax.rem(x + d, nx) for d in range(1, nx)]
    zpeer = [lax.rem(z + d, nz) for d in range(1, nz)]

    barrier = pltpu.get_barrier_semaphore()
    peers = [partner, nxt, prv]
    peers += [at(z, xp, c) for xp in xpeer]
    peers += [at(zp, x, c) for zp in zpeer]
    for p in peers:
        pl.semaphore_signal(barrier, inc=1, device_id={"seq": p})

    def rcopy(src, dst, ss, rs, dev):
        return pltpu.make_async_remote_copy(
            src_ref=src, dst_ref=dst, send_sem=ss, recv_sem=rs, device_id={"seq": dev}
        )

    def lanes_of(k):
        return pl.ds(k * ch, ch)

    smalls = [
        (dt_hbm, dt_ref),
        (dtb_hbm, dtb_ref),
        (alog_hbm, alog_ref),
        (bc_hbm, bc_ref),
        (wx_hbm, wx_ref),
        (bx_hbm, bx_ref),
        (wbc_hbm, wbc_ref),
        (bbc_hbm, bbc_ref),
        (skip_hbm, skip_ref),
    ]
    small_in = [pltpu.make_async_copy(p, q, sem_small.at[i]) for i, (p, q) in enumerate(smalls)]
    xin = [
        pltpu.make_async_copy(x_hbm.at[:, lanes_of(k)], xv.at[:, lanes_of(k)], sem_in.at[k])
        for k in range(nk)
    ]
    zin = pltpu.make_async_copy(z_hbm, zv, sem_in.at[nk])
    for cp in small_in[0:3]:
        cp.start()
    xin[0].start()
    for cp in small_in[3:]:
        cp.start()
    for cp in xin[1:]:
        cp.start()
    zin.start()

    def twice(ref):
        row = jnp.broadcast_to(ref[...], (8, HL))
        return jnp.concatenate([row, row], axis=1)

    for cp in small_in[0:3]:
        cp.wait()
    dtv = dt_ref[...].astype(F32)
    raw = jnp.transpose(jnp.concatenate([dtv, dtv], axis=0)) + twice(dtb_ref)[0:1]
    step = jnp.maximum(raw, 0.0) + jnp.log1p(jnp.exp(-jnp.abs(raw)))
    rate = -jnp.exp(twice(alog_ref)[0:1]) * step
    low = lax.broadcasted_iota(jnp.int32, (T, T), 0) >= lax.broadcasted_iota(jnp.int32, (T, T), 1)
    ld2 = jnp.dot(
        jnp.where(low, 1.0, 0.0),
        rate,
        precision=lax.Precision.HIGHEST,
        preferred_element_type=F32,
    ) * LOG2E
    r2 = ld2 - jnp.log(step) * LOG2E
    last2 = ld2[T - 1 : T, :]
    ldg[0] = ld2
    r2s[...] = r2

    def pair(v):
        hi = v.astype(BF16).astype(F32)
        lane = lax.broadcasted_iota(jnp.int32, v.shape, 1)
        return jnp.where(lane < HL, hi, v - hi).astype(BF16)

    f1s[...] = pair(jnp.exp2(last2 - r2))
    lo_b[...] = jnp.broadcast_to(last2, (8, 2 * HL))

    def make_ex(k):
        @pl.loop(0, ch // 256)
        def _(j):
            base = k * ch + j * 256
            row = lax.broadcasted_iota(jnp.int32, (128, 256), 0) & 63
            head = (lax.broadcasted_iota(jnp.int32, (128, 256), 1) + base) >> 6
            ex[:, pl.ds(pl.multiple_of(base, 256), 256)] = jnp.where(row == head, 1.0, 0.0).astype(BF16)

    pl.semaphore_wait(barrier, len(peers))
    hal = [
        rcopy(x_hbm.at[pl.ds(T - 8, 8), :], halo_x, sem_halo.at[0], sem_halo.at[1], nxt),
        rcopy(bc_hbm.at[pl.ds(T - 8, 8), :], halo_bc, sem_halo.at[2], sem_halo.at[3], nxt),
    ]
    for cp in hal:
        cp.start()
    lcopy = rcopy(lo_b, lp_b, sem_l.at[0], sem_l.at[1], partner)
    lcopy.start()

    def conv_main(src, dst, w_ref, b_ref, lanes):
        v = src[:, lanes].astype(F32)
        acc = b_ref[:, lanes] + w_ref[3:4, lanes] * v
        for k in range(1, 4):
            acc = acc + w_ref[3 - k : 4 - k, lanes] * pltpu.roll(v, k, axis=0)
        dst[:, lanes] = silu(acc).astype(BF16)

    def conv_head(src, halo, w_ref, b_ref, lanes):
        top = jnp.where(me > 0, halo[:, lanes].astype(F32), 0.0)
        v = jnp.concatenate([top, src[0:16, lanes].astype(F32)], axis=0)
        acc = b_ref[:, lanes] + w_ref[3:4, lanes] * v
        for k in range(1, 4):
            acc = acc + w_ref[3 - k : 4 - k, lanes] * pltpu.roll(v, k, axis=0)
        return silu(acc[8:24]).astype(BF16)

    def stage_main(k):
        xin[k].wait()

        @pl.loop(0, ch // 256)
        def _(j):
            conv_main(xv, xc, wx_ref, bx_ref, pl.ds(pl.multiple_of(k * ch + j * 256, 256), 256))

    def stage_head(k):
        lanes = lanes_of(k)
        xc[0:16, lanes] = conv_head(xv, halo_x, wx_ref, bx_ref, lanes)

    whole = pl.ds(0, 2 * N)
    make_ex(0)
    for cp in small_in[3:]:
        cp.wait()
    stage_main(0)
    conv_main(bc_ref, bcs, wbc_ref, bbc_ref, whole)
    make_ex(1)
    stage_main(1)
    stage_main(2 % nk) if nk > 2 else None

    @pl.when(z == 0)
    def _():
        perecv[...] = jnp.zeros_like(perecv)

    for cp in hal:
        cp.wait_recv()
    bcs[0:16, :] = conv_head(bc_ref, halo_bc, wbc_ref, bbc_ref, whole)
    bt[...] = jnp.transpose(bcs[:, 0:N].astype(F32)).astype(BF16)

    first = c == 0

    def stage_decay_l():
        lcopy.wait_recv()
        own = lo_b[...]
        other = lp_b[...]
        l0 = jnp.where(first, own, other)
        l1 = jnp.where(first, other, own)
        cl = l0 + l1
        cl_b[...] = cl
        xd_b[x] = cl
        for d, xp in enumerate(xpeer):
            rcopy(cl_b, xd_b.at[x], sx_s.at[d], sx_r.at[x], at(z, xp, c)).start()
        dl[...] = dot(pair(jnp.concatenate([jnp.exp2(l0), jnp.exp2(l1)], axis=0)), ex[...])

    oh = pl.multiple_of(c * hr, hr)
    ph = pl.multiple_of((1 - c) * hr, hr)

    def d_copy(k):
        return rcopy(
            sbf.at[pl.ds(ph, hr), lanes_of(k)], srecv.at[:, lanes_of(k)], d_s.at[k], d_r.at[k], partner
        )

    def stage_a(k):
        for j in range(ch // 256):
            lanes = pl.ds(k * ch + j * 256, 256)
            f1e = dot(f1s[...], ex[:, lanes])
            weighted = (xc[:, lanes].astype(F32) * f1e).astype(BF16)
            sbf[:, lanes] = dot(bt[...], weighted).astype(BF16)
        d_copy(k).start()

    def x_copy(k, d):
        xp = xpeer[d]
        rows = pl.ds(pl.multiple_of(xp * xr, xr), xr)
        return rcopy(
            csb.at[rows, lanes_of(k)],
            xrecv.at[x, :, lanes_of(k)],
            x_s.at[k, d],
            x_r.at[k, x],
            at(z, xp, c),
        )

    def x_wait(k, d):
        xp = xpeer[d]
        rcopy(
            csb.at[pl.ds(0, xr), lanes_of(k)],
            xrecv.at[xp, :, lanes_of(k)],
            x_s.at[k, d],
            x_r.at[k, xp],
            at(z, xp, c),
        ).wait_recv()

    def stage_b(k):
        d_copy(k).wait_recv()
        lanes = lanes_of(k)
        mine = sbf[pl.ds(oh, hr), lanes].astype(F32)
        got = srecv[:, lanes].astype(F32)
        e1 = dl[8:9, lanes]
        wm = jnp.where(first, e1, 1.0)
        wg = jnp.where(first, 1.0, e1)
        csb[:, lanes] = (wm * mine + wg * got).astype(BF16)
        for d in range(nx - 1):
            x_copy(k, d).start()
        xrecv[x, :, lanes] = csb[pl.ds(pl.multiple_of(x * xr, xr), xr), lanes]

    def zd_copy(o):
        return rcopy(pl_b, zd_b.at[z], sz_s.at[o], sz_r.at[z], at(o, x, c))

    def stage_decay_x():
        for d, xp in enumerate(xpeer):
            rcopy(cl_b, xd_b.at[xp], sx_s.at[d], sx_r.at[xp], at(z, xp, c)).wait_recv()
        rows = [xd_b[i][0:1] for i in range(nx)]
        total = rows[0]
        for i in range(1, nx):
            total = total + rows[i]
        after = []
        run = jnp.zeros_like(rows[0])
        for i in reversed(range(nx)):
            after.insert(0, run)
            run = run + rows[i]
        full = jnp.concatenate(
            after + rows + [jnp.zeros_like(rows[0])] * (16 - 2 * nx), axis=0
        )
        dx[...] = dot(pair(jnp.exp2(full)), ex[...])
        pl_b[...] = jnp.broadcast_to(total, (8, 2 * HL))
        for o in range(no):

            @pl.when(z == o)
            def _():
                zd_b[o] = jnp.broadcast_to(total, (8, 2 * HL))

            @pl.when((z != o) & (z < nz - 1))
            def _():
                zd_copy(o).start()

    def own_lanes(k):
        return pl.ds(k * zw, zw)

    def lanes_to(k, o):
        return pl.ds(k * ch + o * zw, zw)

    def z_copy(k, o):
        return rcopy(
            ptb.at[:, lanes_to(k, o)],
            zrecv.at[z, :, own_lanes(k)],
            z_s.at[k, o],
            z_r.at[k, z],
            at(o, x, c),
        )

    def stage_c(k):
        for d in range(nx - 1):
            x_wait(k, d)
        lanes = lanes_of(k)
        tot = dx[0:1, lanes] * xrecv[0, :, lanes].astype(F32)
        for i in range(1, nx):
            tot = tot + dx[i : i + 1, lanes] * xrecv[i, :, lanes].astype(F32)
        ptb[:, lanes] = tot.astype(BF16)
        for o in range(no):

            @pl.when(z == o)
            def _():
                zrecv[o, :, own_lanes(k)] = ptb[:, lanes_to(k, o)]

            @pl.when((z != o) & (z < nz - 1))
            def _():
                z_copy(k, o).start()

    def zb_copy(k, o, j):
        return rcopy(
            pesend.at[j, :, own_lanes(k)],
            perecv.at[:, lanes_to(k, o)],
            zb_s.at[k, j],
            zb_r.at[k, o],
            at(j, x, c),
        )

    def stage_d():
        lead = [0.0, 0.8, 1.6, 2.5, 4.0, 4.0, 4.1, 4.1]
        order = sorted(
            (lead[min(i, 7)] + 1.1 * k, i, k) for i in range(nz - 1) for k in range(nk)
        )
        for o in range(no):

            @pl.when(z == o)
            def _():
                states = [jnp.zeros((xr, zw), F32) for _ in range(nk)]
                rows = []
                for i in range(nz - 1):
                    if i != o:
                        rcopy(pl_b, zd_b.at[i], sz_s.at[0], sz_r.at[i], at(i, x, c)).wait_recv()
                    rows.append(zd_b[i][0:1])
                full = jnp.concatenate(rows + [rows[0]] * (17 - nz), axis=0)
                full = pair(jnp.exp2(full))
                for q in range(nk):
                    dz[:, q * zw : (q + 1) * zw] = dot(full, ex[:, lanes_to(q, o)])
                for _, i, k in order:
                    if i != o:
                        rcopy(
                            ptb.at[:, pl.ds(0, zw)],
                            zrecv.at[i, :, own_lanes(k)],
                            z_s.at[k, 0],
                            z_r.at[k, i],
                            at(i, x, c),
                        ).wait_recv()
                    old = states[k]
                    new = dz[i : i + 1, own_lanes(k)] * old + zrecv[i, :, own_lanes(k)].astype(F32)
                    states[k] = new
                    if i + 1 == o:
                        perecv[:, lanes_to(k, o)] = new.astype(BF16)
                    else:
                        pesend[i + 1, :, own_lanes(k)] = new.astype(BF16)
                        zb_copy(k, o, i + 1).start()

    def xb_copy(k, d):
        xp = xpeer[d]
        rows = pl.ds(pl.multiple_of(x * xr, xr), xr)
        return rcopy(
            esend.at[xp, :, lanes_of(k)],
            erecv.at[rows, lanes_of(k)],
            xb_s.at[k, d],
            xb_r.at[k, x],
            at(z, xp, c),
        )

    def stage_e(k):
        for o in range(no):

            @pl.when((z != o) & (z > 0))
            def _():
                rcopy(
                    pesend.at[0, :, own_lanes(k)],
                    perecv.at[:, lanes_to(k, o)],
                    zb_s.at[k, 0],
                    zb_r.at[k, o],
                    at(o, x, c),
                ).wait_recv()

        lanes = lanes_of(k)
        state = perecv[:, lanes].astype(F32)
        for i in range(nx):
            esend[i, :, lanes] = state.astype(BF16)
            if i < nx - 1:
                state = dx[nx + i : nx + i + 1, lanes] * state + xrecv[i, :, lanes].astype(F32)
        for d in range(nx - 1):
            xb_copy(k, d).start()
        erecv[pl.ds(pl.multiple_of(x * xr, xr), xr), lanes] = esend[x, :, lanes]

    def db_copy(k):
        return rcopy(
            entsend.at[:, lanes_of(k)],
            ent.at[pl.ds(oh, hr), lanes_of(k)],
            db_s.at[k],
            db_r.at[k],
            partner,
        )

    def stage_f(k):
        lanes = lanes_of(k)
        for d, xp in enumerate(xpeer):
            rows = pl.ds(pl.multiple_of(xp * xr, xr), xr)
            rcopy(
                esend.at[xp, :, lanes],
                erecv.at[rows, lanes],
                xb_s.at[k, d],
                xb_r.at[k, xp],
                at(z, xp, c),
            ).wait_recv()
        e0 = erecv[:, lanes]
        mine = sbf[pl.ds(oh, hr), lanes]
        got = srecv[:, lanes]
        s0 = jnp.where(first, mine, got).astype(F32)
        e1 = (dl[0:1, lanes] * e0.astype(F32) + s0).astype(BF16)
        entsend[:, lanes] = jnp.where(first, e1, e0)
        db_copy(k).start()
        ent[pl.ds(oh, hr), lanes] = jnp.where(first, e0, e1)

    def prepare():
        cm[...] = bcs[:, N : 2 * N]
        base = ldg[0]
        for g in range(1, ngroup):
            ldg[g] = pltpu.roll(base, 128 - 8 * g, axis=1)
        rt[...] = jnp.transpose(r2s[...])
        f2s[...] = pair(jnp.exp2(base))
        skipd = twice(skip_ref)
        skw[...] = dot(pair(jnp.concatenate([skipd, skipd], 0)), ex[...])[0:8]
        s = lax.dot_general(
            cm[...], bcs[:, 0:N], (((1,), (1,)), ((), ())), preferred_element_type=F32
        )
        low_mask = lax.broadcasted_iota(jnp.int32, (T, T), 0) >= lax.broadcasted_iota(
            jnp.int32, (T, T), 1
        )
        sc[...] = jnp.where(low_mask, s, 0.0)

    hb = T // 2

    def mix_group(g):
        ldt = ldg[g]
        rtile = rt[pl.ds(pl.multiple_of(g * 8, 8), 8), :]
        for j in range(4):
            lanes = pl.ds(pl.multiple_of(g * 512 + j * 128, 128), 128)
            xp = xc[:, lanes]
            lane = lax.broadcasted_iota(jnp.int32, (T, 128), 1)
            xa = jnp.where(lane < 64, xp.astype(F32), 0.0).astype(BF16)
            xb = jnp.where(lane >= 64, xp.astype(F32), 0.0).astype(BF16)
            tops = []
            bots = []
            for a in range(2):
                i = 2 * j + a
                col = ldt[:, i : i + 1]
                row = rtile[i : i + 1, :]
                tl = jnp.exp2(jnp.minimum(col[0:hb] - row[:, 0:hb], 126.0)) * sc[0:hb, 0:hb]
                bl = jnp.exp2(col[hb:T] - row[:, 0:hb]) * sc[hb:T, 0:hb]
                br = jnp.exp2(jnp.minimum(col[hb:T] - row[:, hb:T], 126.0)) * sc[hb:T, hb:T]
                tops.append(tl.astype(BF16))
                bots += [bl.astype(BF16), br.astype(BF16)]
            yt = dot(jnp.concatenate(tops, 1), jnp.concatenate([xa[0:hb], xb[0:hb]], 0))
            yb = dot(jnp.concatenate(bots, 1), jnp.concatenate([xa, xb], 0))
            sk = skw[0:1, lanes] * xp.astype(F32)
            inside[0:hb, lanes] = yt + sk[0:hb]
            inside[hb:T, lanes] = yb + sk[hb:T]

    def silu_group(g):
        lanes = pl.ds(g * 512, 512)
        zs[:, lanes] = silu(zv[:, lanes].astype(F32))

    def stage_g(k):
        db_copy(k).wait_recv()

        @pl.loop(0, ch // 256)
        def _(j):
            lanes = pl.ds(pl.multiple_of(k * ch + j * 256, 256), 256)
            f2e = dot(f2s[...], ex[:, lanes])
            y = (inside[:, lanes] + f2e * dot(cm[...], ent[:, lanes])).astype(BF16)
            gated = y.astype(F32) * zs[:, lanes]
            inside[:, lanes] = gated
            sq = gated * gated
            ssq[...] += sq[:, 0:128] + sq[:, 128:256]

    fill = [functools.partial(mix_group, g) for g in range(ngroup)]
    fill += [functools.partial(silu_group, g) for g in range(ngroup)]

    def filler(n):
        for _ in range(n):
            if fill:
                fill.pop(0)()

    stage_head(0)
    stage_a(0)
    stage_head(1)
    stage_a(1)
    for k in range(2, nk):
        make_ex(k)
    stage_decay_l()
    stage_b(0)
    for k in range(2, nk):
        if k > 2:
            stage_main(k)
        stage_head(k)
        stage_a(k)
        stage_b(k - 1)
    stage_decay_x()
    stage_b(nk - 1)
    prepare()
    ssq[...] = jnp.zeros_like(ssq)
    zin.wait()

    for s in range(nk):
        stage_c(s)
        filler(1)
    filler(6)
    stage_d()
    while fill:
        filler(1)
    for s in range(nk):
        stage_e(s)
    stage_f(0)
    for s in range(1, nk):
        stage_f(s)
        stage_g(s - 1)
    stage_g(nk - 1)

    ms = jnp.sum(ssq[...], axis=1, keepdims=True) * (1.0 / di)
    rs_ref[...] = jnp.broadcast_to(lax.rsqrt(ms + 1e-05), (T, 128))

    for cp in hal:
        cp.wait_send()
    lcopy.wait_send()
    for d, xp in enumerate(xpeer):
        rcopy(cl_b, xd_b.at[x], sx_s.at[d], sx_r.at[x], at(z, xp, c)).wait_send()
    for o in range(no):

        @pl.when((z != o) & (z < nz - 1))
        def _():
            zd_copy(o).wait_send()
            for k in range(nk):
                z_copy(k, o).wait_send()

        @pl.when(z == o)
        def _():
            for k in range(nk):
                for j in range(1, nz):
                    if j != o:
                        zb_copy(k, o, j).wait_send()

    for k in range(nk):
        d_copy(k).wait_send()
        db_copy(k).wait_send()
        for d in range(nx - 1):
            x_copy(k, d).wait_send()
            xb_copy(k, d).wait_send()


def norm_kernel(gated, scale, gain_hbm, out_hbm, ov, gain, sem_in, sem_out):
    di = gated.shape[1]
    quarter = di // 4
    cp = pltpu.make_async_copy(gain_hbm, gain, sem_in.at[0])
    cp.start()
    cp.wait()
    outs = []
    for i in range(4):

        @pl.loop(0, quarter // 128)
        def _(j):
            lanes = pl.ds(pl.multiple_of(i * quarter + j * 128, 128), 128)
            ov[:, lanes] = (gated[:, lanes] * scale[...] * gain[:, lanes]).astype(BF16)

        lanes = pl.ds(i * quarter, quarter)
        out = pltpu.make_async_copy(ov.at[:, lanes], out_hbm.at[:, lanes], sem_out.at[i])
        out.start()
        outs.append(out)
    for out in outs:
        out.wait()


def make_body(nz, nx, nk, no):
    def body(x_raw, z_gate, bc_raw, dt_raw, wx, bx, wbc, bbc, dtb, alog, skip, gain):
        di = x_raw.shape[1]
        ch = di // nk
        zw = ch // no
        hr = N // 2
        xr = hr // nx
        ng = di // 512
        vm = lambda *s: pltpu.VMEM(s, F32)
        vb = lambda *s: pltpu.VMEM(s, BF16)
        dma = lambda *s: pltpu.SemaphoreType.DMA(s)
        anyspec = pl.BlockSpec(memory_space=pltpu.HBM)
        scratch = [
            vb(T, 2 * N),
            vb(HL, T),
            vm(4, di),
            vm(1, di),
            vm(4, 2 * N),
            vm(1, 2 * N),
            vm(1, HL),
            vm(1, HL),
            vm(1, HL),
            vb(T, 2 * N),
            vm(T, di),
            vb(T, di),
            vb(T, di),
            vb(T, di),
            vb(8, di),
            vb(8, 2 * N),
            vm(T, 128),
            vb(128, di),
            vm(ng, T, 128),
            vm(128, T),
            vb(T, 128),
            vb(T, 128),
            vb(N, T),
            vb(T, N),
            vm(T, T),
            vm(8, di),
            vm(T, 128),
            vm(8, 128),
            vm(8, 128),
            vm(8, 128),
            vm(nx, 8, 128),
            vm(8, 128),
            vm(nz, 8, 128),
            vm(16, di),
            vm(16, di),
            vm(16, nk * zw),
            vb(N, di),
            vb(hr, di),
            vb(hr, di),
            vb(nx, xr, di),
            vb(xr, di),
            vb(nz, xr, nk * zw),
            vb(nz, xr, nk * zw),
            vb(xr, di),
            vb(nx, xr, di),
            vb(hr, di),
            vb(hr, di),
            vb(N, di),
            dma(nk + 1),
            dma(9),
            dma(4),
            dma(2),
            dma(nx),
            dma(nx),
            dma(nz),
            dma(nz),
            dma(nk),
            dma(nk),
            dma(nk, nx),
            dma(nk, nx),
            dma(nk, nz),
            dma(nk, nz),
            dma(nk, nz),
            dma(nk, nz),
            dma(nk, nx),
            dma(nk, nx),
            dma(nk),
            dma(nk),
        ]
        gated, scale = pl.pallas_call(
            functools.partial(kernel, nz, nx, di, nk, no),
            out_shape=(
                pltpu.VMEM((T, di), F32),
                pltpu.VMEM((T, 128), F32),
            ),
            in_specs=[anyspec] * 11,
            out_specs=(pl.BlockSpec(memory_space=pltpu.VMEM),) * 2,
            scratch_shapes=scratch,
            compiler_params=pltpu.CompilerParams(
                collective_id=0, has_side_effects=True, vmem_limit_bytes=48 * 1024 * 1024
            ),
        )(
            *(
                pltpu.with_memory_space_constraint(a, pltpu.HBM)
                for a in (
            x_raw,
            z_gate,
            bc_raw,
            dt_raw.T,
            wx,
            bx.reshape(1, -1),
            wbc,
            bbc.reshape(1, -1),
            dtb.reshape(1, -1),
            alog.reshape(1, -1),
            skip.reshape(1, -1),
                )
            )
        )
        full = pl.BlockSpec(memory_space=pltpu.VMEM)
        return pl.pallas_call(
            norm_kernel,
            out_shape=jax.ShapeDtypeStruct((T, di), BF16),
            in_specs=[full, full, anyspec],
            out_specs=anyspec,
            scratch_shapes=[vb(T, di), vm(1, di), dma(1), dma(4)],
            compiler_params=pltpu.CompilerParams(vmem_limit_bytes=16 * 1024 * 1024),
        )(gated, scale, pltpu.with_memory_space_constraint(gain.reshape(1, -1), pltpu.HBM))

    return body


def solution(mesh):
    nx = 4
    nz = mesh.shape["seq"] // (2 * nx)
    tok = P(("vol", "seq"), None)
    return jax.shard_map(
        make_body(nz, nx, 4, 4),
        mesh=mesh,
        in_specs=(tok, tok, tok, tok) + (P(),) * 8,
        out_specs=tok,
        check_vma=False,
    )
```
